128 devices in a mesh: rows: 16 (over x, z_hi, core), cols: 8 (over y, z_lo).
Axes of the slice: x: 4, y: 4, z: 4 (z_hi: 2, z_lo: 2; z = z_hi * 2 + z_lo), core: 2. Of those that a mesh axis runs over, the one named last changes fastest.
Arguments:
- bottleneck: bfloat16 [8, 256, 16, 256], P(None, None, 'rows', 'cols'), may hold values from -8 to 8
- skip_field: bfloat16 [8, 128, 32, 512], P(None, None, 'rows', 'cols'), may hold values from -6 to 6
- cotangent: bfloat16 [8, 128, 32, 512], P(None, None, 'rows', 'cols'), may hold values from -6 to 6
- noise_level: int32 [8], replicated, may hold values from 0 to 17
- qkv_weight: bfloat16 [768, 256], replicated, may hold values from -0.5 to 0.5
- out_weight: bfloat16 [256, 256], replicated, may hold values from -3 to 3
- up_weight: bfloat16 [128, 256], replicated, may hold values from -0.375 to 0.375
- conv_weight: bfloat16 [9, 128, 128], replicated, may hold values from -0.1875 to 0.1875
- film_scale: float32 [18, 128], replicated, may hold values from -2 to 2
- film_shift: float32 [18, 128], replicated, may hold values from -2 to 2
Outputs:
- decoded: bfloat16 [8, 128, 32, 512], P(None, None, 'rows', 'cols')
- grad_bottleneck: float32 [8, 256, 16, 256], P(None, None, 'rows', 'cols')
- grad_skip: bfloat16 [8, 128, 32, 512], P(None, None, 'rows', 'cols')
- grad_qkv: float32 [768, 256], replicated
- grad_out: float32 [256, 256], replicated
- grad_up: float32 [128, 256], replicated
- grad_conv: float32 [9, 128, 128], replicated
- grad_scale: float32 [18, 128], replicated
- grad_shift: float32 [18, 128], replicated
The draws below stay inside these ranges and needn't reach their ends.
All inputs are finite; a program needn't handle non-finite values.
Results may differ from the reference program's by a relative error of at most 0.023.
The reference program's roundings to bfloat16 on the way count: a program that leaves them out, or rounds other values in their place, can miss the bound.
Values may be sent and summed in bfloat16 or wider, within the bound.
A program may use at most 64 MiB of HBM per device.

```python
import math
import jax
import jax.numpy as jnp
from jax import lax

C4 = 256
C3 = 128
HEAD_DIM = 64
LEVELS = 18
BATCH = 8
H4N = 16
W4N = 256
H3N = 32
W3N = 512


def draw_bottleneck(key, part):
    base = jax.random.normal(key, (BATCH, C4, H4N, W4N), jnp.float32)
    return jnp.clip(base, -8.0, 8.0).astype(jnp.bfloat16)


def plant(drawn, rng, low, high):
    spot = [jax.random.randint(jax.random.fold_in(rng, axis), (), 0, length) for axis, length in enumerate(drawn.shape)]
    longest = drawn.shape.index(max(drawn.shape))
    beside = spot[:longest] + [(spot[longest] + 1) % drawn.shape[longest]] + spot[longest + 1:]
    return drawn.at[tuple(spot)].set(low).at[tuple(beside)].set(high)


def levels(key, extent, shards, smallest, top_value):
    gain = 1.0
    for axis_at, parts in shards:
        heights = jax.random.uniform(jax.random.fold_in(jax.random.fold_in(key, 6), axis_at), (parts,), jnp.float32, smallest / len(shards), top_value / len(shards))
        gain = gain * jnp.repeat(jnp.exp(heights), extent[axis_at] // parts).reshape((-1,) + (1,) * (len(extent) - 1 - axis_at))
    return gain


def bell_draw(rng, extent, scale, bound, shards=(), kind=jnp.bfloat16):
    values = jax.random.normal(rng, extent, jnp.float32) * scale
    if len(shards) > 0:
        values = levels(rng, extent, shards, -0.22, 0.18) * values
    return jnp.clip(values, min=-bound, max=bound).astype(kind)


def setup_inputs(seed: int = 0) -> dict:
    seeds = jax.random.split(jax.random.key(seed), 11)
    bottleneck = draw_bottleneck(jax.random.fold_in(seeds[10], 71), 0)
    skip_field = bell_draw(seeds[1], (BATCH, C3, H3N, W3N), 1.0, 6.0, ((2, 16), (3, 8)))
    cotangent = bell_draw(seeds[2], (BATCH, C3, H3N, W3N), 1.0, 6.0, ((2, 16), (3, 8)))
    noise_level = plant(jax.random.randint(seeds[3], (BATCH,), 0, LEVELS), jax.random.fold_in(seeds[3], 1), 0, LEVELS - 1).astype(jnp.int32)
    qkv_weight = bell_draw(seeds[4], (3 * C4, C4), (C4 // 2) ** -0.5, 0.5)
    out_weight = bell_draw(seeds[5], (C4, C4), (max(C4 // 64, 1)) ** -0.5, 3.0)
    up_weight = bell_draw(seeds[6], (C3, C4), C4 ** -0.5, 0.375)
    conv_weight = bell_draw(seeds[7], (9, C3, C3), (9 * C3) ** -0.5, 0.1875)
    film_scale = bell_draw(seeds[8], (LEVELS, C3), 0.5, 2.0, (), jnp.float32)
    film_shift = bell_draw(seeds[9], (LEVELS, C3), 0.5, 2.0, (), jnp.float32)
    return {"bottleneck": bottleneck, "skip_field": skip_field, "cotangent": cotangent, "noise_level": noise_level, "qkv_weight": qkv_weight, "out_weight": out_weight, "up_weight": up_weight, "conv_weight": conv_weight, "film_scale": film_scale, "film_shift": film_shift}


OFFSETS = [(-1, -1), (-1, 0), (-1, 1), (0, -1), (0, 0), (0, 1), (1, -1), (1, 0), (1, 1)]

def rounded(value):
    return lax.optimization_barrier(value.astype(jnp.bfloat16)).astype(jnp.float32)

def reference(bottleneck, skip_field, cotangent, noise_level, qkv_weight, out_weight, up_weight, conv_weight, film_scale, film_shift):
    heads = C4 // HEAD_DIM
    tokens = H4N * W4N
    factor = 1.0 / math.sqrt(HEAD_DIM)
    highest = lax.Precision.HIGHEST
    onehot = (noise_level[:, None] == jnp.arange(LEVELS, dtype=jnp.int32)[None, :]).astype(jnp.float32)
    scale_rows = 1.0 + jnp.dot(onehot, film_scale, precision=highest)
    shift_rows = jnp.dot(onehot, film_shift, precision=highest)
    starts = jnp.arange(H4N, dtype=jnp.int32) * W4N
    conv_float = conv_weight.astype(jnp.float32)

    def one_sample(inputs):
        field, skip_one, grad_one, scale_one, shift_one = inputs
        matrix = field.reshape(C4, tokens)
        projected = jnp.dot(qkv_weight, matrix, preferred_element_type=jnp.float32).astype(jnp.bfloat16)
        split = projected.reshape(3, heads, HEAD_DIM, tokens).astype(jnp.float32)
        queries, key_rows, value_rows = (split[0], split[1], split[2])

        def forward_block(start):
            query_block = lax.dynamic_slice_in_dim(queries, start, W4N, 2)
            scores = jnp.einsum('hdi,hdj->hij', query_block, key_rows) * factor
            highest_score = lax.optimization_barrier(jnp.max(scores, axis=2))
            powers = jnp.exp(scores - highest_score[:, :, None])
            total = lax.optimization_barrier(jnp.sum(powers, axis=2))
            attend = rounded(powers / total[:, :, None])
            mixed = jnp.einsum('hij,hdj->hdi', attend, value_rows).astype(jnp.bfloat16)
            return (mixed, highest_score, total)
        mixed, top_rows, total_rows = lax.map(forward_block, starts)
        attended = mixed.transpose(1, 2, 0, 3).reshape(heads, HEAD_DIM, tokens)
        top_all = top_rows.transpose(1, 0, 2).reshape(heads, tokens)
        total_all = total_rows.transpose(1, 0, 2).reshape(heads, tokens)
        flat = attended.reshape(C4, tokens)
        branch = jnp.dot(out_weight, flat, preferred_element_type=jnp.float32)
        updated = (matrix.astype(jnp.float32) + branch).astype(jnp.bfloat16)
        lifted = jnp.dot(up_weight, updated, preferred_element_type=jnp.float32).reshape(C3, H4N, W4N)
        lifted = jnp.repeat(jnp.repeat(lifted, 2, axis=1), 2, axis=2)
        summed = lifted + skip_one.astype(jnp.float32)
        active = summed * scale_one[:, None, None] + shift_one[:, None, None]
        sigmoid = jax.nn.sigmoid(active)
        hidden = (active * sigmoid).astype(jnp.bfloat16)
        padded = jnp.pad(hidden, ((0, 0), (1, 1), (1, 1))).astype(jnp.float32)
        grad_pad = jnp.pad(grad_one, ((0, 0), (1, 1), (1, 1))).astype(jnp.float32)
        result = jnp.zeros((C3, H3N, W3N), jnp.float32)
        grad_hidden = jnp.zeros((C3, H3N, W3N), jnp.float32)
        conv_terms = []
        for number, (row_step, col_step) in enumerate(OFFSETS):
            window = padded[:, 1 + row_step:1 + row_step + H3N, 1 + col_step:1 + col_step + W3N]
            result = result + jnp.einsum('oc,chw->ohw', conv_float[number], window)
            shifted = grad_pad[:, 1 - row_step:1 - row_step + H3N, 1 - col_step:1 - col_step + W3N]
            grad_hidden = grad_hidden + jnp.einsum('oc,ohw->chw', conv_float[number], shifted)
            conv_terms.append(jnp.einsum('ohw,chw->oc', grad_one.astype(jnp.float32), window))
        decoded = result.astype(jnp.bfloat16)
        slope = sigmoid * (1.0 + active * (1.0 - sigmoid))
        grad_active = grad_hidden * slope
        grad_summed = grad_active * scale_one[:, None, None]
        scale_term = lax.optimization_barrier(jnp.sum(grad_active * summed, axis=(1, 2)))
        shift_term = lax.optimization_barrier(jnp.sum(grad_active, axis=(1, 2)))
        grad_skip = grad_summed.astype(jnp.bfloat16)
        coarse = grad_summed.reshape(C3, H4N, 2, W4N, 2).sum(axis=(2, 4)).astype(jnp.bfloat16).reshape(C3, tokens)
        up_term = jnp.dot(coarse, updated.T, preferred_element_type=jnp.float32)
        grad_lifted = jnp.dot(up_weight.T, coarse, preferred_element_type=jnp.float32)
        grad_low = grad_lifted.astype(jnp.bfloat16)
        out_term = jnp.dot(grad_low, flat.T, preferred_element_type=jnp.float32)
        grad_attended = jnp.dot(out_weight.T, grad_low, preferred_element_type=jnp.float32).astype(jnp.bfloat16)
        grad_float = grad_attended.reshape(heads, HEAD_DIM, tokens).astype(jnp.float32)
        deltas = lax.optimization_barrier(jnp.sum(grad_float * attended.astype(jnp.float32), axis=1))

        def backward_block(carry, start):
            key_grad, value_grad = carry
            query_block = lax.dynamic_slice_in_dim(queries, start, W4N, 2)
            grad_block = lax.dynamic_slice_in_dim(grad_float, start, W4N, 2)
            top_block = lax.dynamic_slice_in_dim(top_all, start, W4N, 1)
            total_block = lax.dynamic_slice_in_dim(total_all, start, W4N, 1)
            delta_block = lax.dynamic_slice_in_dim(deltas, start, W4N, 1)
            scores = jnp.einsum('hdi,hdj->hij', query_block, key_rows) * factor
            probs = jnp.exp(scores - top_block[:, :, None]) / total_block[:, :, None]
            value_grad = value_grad + jnp.einsum('hij,hdi->hdj', rounded(probs), grad_block)
            dots = jnp.einsum('hdi,hdj->hij', grad_block, value_rows)
            score_grad = rounded(probs * (dots - delta_block[:, :, None]))
            query_grad = jnp.einsum('hij,hdj->hdi', score_grad, key_rows) * factor
            key_grad = key_grad + jnp.einsum('hij,hdi->hdj', score_grad, query_block) * factor
            return ((key_grad, value_grad), query_grad)
        empty = jnp.zeros((heads, HEAD_DIM, tokens), jnp.float32)
        (key_grad, value_grad), query_parts = lax.scan(backward_block, (empty, empty), starts)
        query_grad = query_parts.transpose(1, 2, 0, 3).reshape(heads, HEAD_DIM, tokens)
        stacked = jnp.stack([query_grad, key_grad, value_grad]).reshape(3 * C4, tokens).astype(jnp.bfloat16)
        qkv_term = jnp.dot(stacked, matrix.T, preferred_element_type=jnp.float32)
        grad_input = grad_lifted + jnp.dot(qkv_weight.T, stacked, preferred_element_type=jnp.float32)
        return (decoded, grad_input.reshape(C4, H4N, W4N), grad_skip, qkv_term, out_term, up_term, jnp.stack(conv_terms), scale_term, shift_term)
    outputs = lax.map(one_sample, (bottleneck, skip_field, cotangent, scale_rows, shift_rows))
    decoded, grad_bottleneck, grad_skip, qkv_terms, out_terms, up_terms, conv_terms, scale_terms, shift_terms = outputs
    grad_scale = jnp.dot(onehot.T, scale_terms, precision=highest)
    grad_shift = jnp.dot(onehot.T, shift_terms, precision=highest)
    return (decoded, grad_bottleneck, grad_skip, lax.optimization_barrier(jnp.sum(qkv_terms, axis=0)), lax.optimization_barrier(jnp.sum(out_terms, axis=0)), lax.optimization_barrier(jnp.sum(up_terms, axis=0)), lax.optimization_barrier(jnp.sum(conv_terms, axis=0)), grad_scale, grad_shift)
```

```python
import functools

import jax
import jax.numpy as jnp
from jax import lax
from jax.experimental import pallas as pl
from jax.experimental.pallas import tpu as pltpu
from jax.sharding import PartitionSpec as P

MESH = pl.DeviceIdType.MESH
BF = jnp.bfloat16
F32 = jnp.float32
ROWS, COLS = 16, 8
HEADS = 4
BLOCK = 256
CHUNK = 1024
TAPS = [(-1, -1), (-1, 0), (-1, 1), (0, -1), (0, 0), (0, 1), (1, -1), (1, 0), (1, 1)]
VMEM = pl.BlockSpec(memory_space=pltpu.VMEM)


def nn(a, b):
    return lax.dot_general(a, b, (((1,), (0,)), ((), ())), preferred_element_type=F32)


def nt(a, b):
    return lax.dot_general(a, b, (((1,), (1,)), ((), ())), preferred_element_type=F32)


def remote(src, dst, send, recv, row, col):
    return pltpu.make_async_remote_copy(
        src_ref=src, dst_ref=dst, send_sem=send, recv_sem=recv, device_id=(row, col), device_id_type=MESH
    )


def send_or_keep(here, src, dst, send, recv, row, col):
    @pl.when(here)
    def _():
        pltpu.make_async_copy(src, dst, recv).start()

    @pl.when(jnp.logical_not(here))
    def _():
        remote(src, dst, send, recv, row, col).start()


def drain(ref, sem):
    pltpu.make_async_copy(ref, ref, sem).wait()


def loop(lo, hi, body):
    def step(i, carry):
        body(i)
        return carry

    lax.fori_loop(lo, hi, step, 0)


def kernel(
    x_ref, skip_ref, cot_ref, noise_col, noise_row, wqkv, woutn, wup, wconv, fscale, fshift,
    dec_ref, gb_ref, gskip_ref, gqkv_ref, gout_ref, gup_ref, gconv_ref, gscale_ref, gshift_ref,
    wq, wkv, kv_send, q_send, kv_in, q_in, v1, s_ref, p_ref, invl_ref, o_buf, ocell,
    gx, hx, gt, gedge, hedge, ghalo, hhalo, pre_ref, act_ref, dh_ref, y_ref, dy_ref, du_ref,
    do_send, do_in, dkvt, dq_buf, dq_in, pair_send, pair_in, dkv_send, dkv_in, gacc,
    eg, epin, ehs, ersin, eag, lg, lpin, lhs, lrsin, lag, sems,
):
    r, c = lax.axis_index("rows"), lax.axis_index("cols")
    me = r * COLS + c
    par = lax.rem(r, 2)
    mate = r + 1 - 2 * par
    kslot = lax.div(r, 2) * COLS + c
    head, quarter = lax.div(r, 4), lax.rem(r, 4)
    qslot = quarter * COLS + c
    own = head == quarter
    pair_index = c * HEADS + head

    barrier = pltpu.get_barrier_semaphore()

    def signal(i):
        d = lax.rem(me + i, ROWS * COLS)
        pl.semaphore_signal(
            barrier, inc=1, device_id=(lax.div(d, COLS), lax.rem(d, COLS)), device_id_type=MESH
        )

    loop(1, ROWS * COLS, signal)

    def to_attention(src, dst, send, recv):
        def one(i):
            k = lax.rem(head * COLS + c + i, 32)
            h, dc = lax.div(k, COLS), lax.rem(k, COLS)
            dr = 4 * h + head
            here = (dr == r) & (dc == c)
            send_or_keep(here, src.at[dc * HEADS + h], dst.at[qslot], send, recv, dr, dc)

        loop(0, 32, one)

    def to_cells(src, dst, send, recv, row):
        def one(i):
            dc = lax.rem(c + i, COLS)
            dr = 4 * quarter + row
            here = (dr == r) & (dc == c)
            send_or_keep(here, src.at[row * COLS + dc], dst.at[pair_index], send, recv, dr, dc)

        loop(0, COLS, one)

    def drain32(ref, sem):
        @pl.when(own)
        def _():
            drain(ref.at[pl.ds(0, 31)], sem)

        @pl.when(jnp.logical_not(own))
        def _():
            drain(ref, sem)

    def parity_device(k):
        return 2 * lax.div(k, COLS) + par, lax.rem(k, COLS)

    def halo_start(ext, edge, halo, base):
        up, down = lax.rem(r + ROWS - 1, ROWS), lax.rem(r + 1, ROWS)
        left, right = lax.rem(c + COLS - 1, COLS), lax.rem(c + 1, COLS)
        copies = [
            remote(ext.at[:, 1, pl.ds(1, 2)], ext.at[:, 3, pl.ds(1, 2)], sems.at[base], sems.at[base + 1], up, c),
            remote(ext.at[:, 2, pl.ds(1, 2)], ext.at[:, 0, pl.ds(1, 2)], sems.at[base + 2], sems.at[base + 3], down, c),
        ]
        at = base + 4
        for row, slot in ((up, 2), (r, 1), (down, 0)):
            copies.append(remote(edge.at[0], halo.at[1, slot], sems.at[at], sems.at[at + 1], row, left))
            copies.append(remote(edge.at[1], halo.at[0, slot], sems.at[at + 2], sems.at[at + 3], row, right))
            at += 4
        for copy in copies:
            copy.start()
        return copies

    def halo_finish(ext, halo, copies):
        for copy in copies:
            copy.wait()

        @pl.when(r == 0)
        def _():
            ext[:, 0, 1:3] = jnp.zeros((8, 2, 32, 128), BF)
            halo[:, 0] = jnp.zeros((2, 2, 8, 128), F32)

        @pl.when(r == ROWS - 1)
        def _():
            ext[:, 3, 1:3] = jnp.zeros((8, 2, 32, 128), BF)
            halo[:, 2] = jnp.zeros((2, 2, 8, 128), F32)

        @pl.when(c == 0)
        def _():
            halo[0] = jnp.zeros((3, 2, 8, 128), F32)

        @pl.when(c == COLS - 1)
        def _():
            halo[1] = jnp.zeros((3, 2, 8, 128), F32)

        place = lax.broadcasted_iota(jnp.int32, (32, 128), 0)

        def one(s):
            for row, (slot, a) in enumerate(((0, 1), (1, 0), (1, 1), (2, 0))):
                odd = ext[s, row, 2].astype(F32)
                even = ext[s, row, 1].astype(F32)
                before = halo[0, slot, a, pl.ds(s, 1), :]
                after = halo[1, slot, a, pl.ds(s, 1), :]
                ext[s, row, 0] = jnp.where(place == 0, before, pltpu.roll(odd, 1, axis=0)).astype(BF)
                ext[s, row, 3] = jnp.where(place == 31, after, pltpu.roll(even, 31, axis=0)).astype(BF)

        loop(0, 8, one)

    class Total:
        def __init__(self, count, g, pin, hs, rsin, ag, base):
            self.count, self.g, self.pin, self.hs, self.rsin, self.ag = count, g, pin, hs, rsin, ag
            self.sem = [sems.at[base + i] for i in range(8)]
            self.reducer = kslot < count

        def start(self):
            remote(self.g.at[1 - par], self.pin, self.sem[0], self.sem[1], mate, c).start()

        def scatter(self):
            remote(self.g.at[1 - par], self.pin, self.sem[0], self.sem[1], mate, c).wait()
            self.hs[...] = (self.g[par].astype(F32) + self.pin[...].astype(F32)).astype(BF)

            def one(i):
                k = lax.rem(kslot + i, self.count)
                dr, dc = parity_device(k)
                send_or_keep(k == kslot, self.hs.at[k], self.rsin.at[kslot], self.sem[2], self.sem[3], dr, dc)

            loop(0, self.count, one)

        def gather(self):
            @pl.when(self.reducer)
            def _():
                drain(self.rsin, self.sem[3])
                self.ag[par, kslot] = jnp.sum(self.rsin[...].astype(F32), axis=0).astype(BF)

                def one(i):
                    dr, dc = parity_device(lax.rem(kslot + i, 64))
                    remote(
                        self.ag.at[par, kslot], self.ag.at[par, kslot], self.sem[4], self.sem[5], dr, dc
                    ).start()

                loop(1, 64, one)

        def swap(self):
            @pl.when(self.reducer)
            def _():
                drain(self.ag.at[0, pl.ds(0, self.count - 1)], self.sem[5])
                drain(self.rsin.at[pl.ds(0, 63)], self.sem[4])
                drain(self.hs.at[pl.ds(0, self.count - 1)], self.sem[2])

            @pl.when(jnp.logical_not(self.reducer))
            def _():
                drain(self.ag.at[0, pl.ds(0, self.count)], self.sem[5])
                drain(self.hs, self.sem[2])

            remote(self.ag.at[par], self.ag.at[par], self.sem[6], self.sem[7], mate, c).start()

        def finish(self):
            remote(self.ag.at[par], self.ag.at[par], self.sem[6], self.sem[7], mate, c).wait()

        def put(self, at, value):
            n = value.shape[0] // 16
            half, k = at // self.count, at % self.count
            self.g[half, k : k + n] = value.astype(BF).reshape(n, 16, 128)

        def get(self, at, n):
            half, k = at // self.count, at % self.count
            return self.ag[half, k : k + n].reshape(n * 16, 128).astype(F32)

    early = Total(64, eg, epin, ehs, ersin, eag, 48)
    late = Total(48, lg, lpin, lhs, lrsin, lag, 56)

    zero64 = jnp.zeros((64, 256), BF)
    for h in range(HEADS):
        wq[128 * h : 128 * h + 64] = (wqkv[64 * h : 64 * h + 64].astype(F32) * 0.125).astype(BF)
        wq[128 * h + 64 : 128 * h + 128] = zero64
        wkv[128 * h : 128 * h + 64] = wqkv[256 + 64 * h : 320 + 64 * h]
        wkv[128 * h + 64 : 128 * h + 128] = wqkv[512 + 64 * h : 576 + 64 * h]
    xt = x_ref[...].reshape(256, 256)
    for h in range(HEADS):
        rows = slice(128 * h, 128 * h + 128)
        kv = nt(xt, wkv[rows, :]).astype(BF).reshape(8, 32, 128)
        q = nt(xt, wq[rows, :]).astype(BF).reshape(8, 32, 128)
        for s in range(8):
            kv_send[s * HEADS + h] = kv[s]
            q_send[s * HEADS + h] = q[s]

    to = lax.broadcasted_iota(jnp.int32, (128, 128), 0)
    of = lax.broadcasted_iota(jnp.int32, (128, 128), 1)
    split = (of == (lax.div(to, 64) * 64 + 2 * lax.rem(to, 32) + lax.rem(lax.div(to, 32), 2))).astype(BF)
    merge = (to == (lax.div(of, 64) * 64 + 2 * lax.rem(of, 32) + lax.rem(lax.div(of, 32), 2))).astype(BF)
    eye = (to == of).astype(BF)

    def take_cot(s):
        g = nn(split, cot_ref[s])
        low = g.astype(BF)
        gx[s, 1:3, 1:3] = low.reshape(2, 2, 32, 128)
        gt[s] = nt(eye, low).astype(BF)
        for a in range(2):
            gedge[0, a, pl.ds(s, 1), :] = g[64 * a : 64 * a + 1]
            gedge[1, a, pl.ds(s, 1), :] = g[64 * a + 63 : 64 * a + 64]

    loop(0, 8, take_cot)

    pl.semaphore_wait(barrier, ROWS * COLS - 1)

    def send_kv(i):
        k = lax.rem(kslot + i, 64)
        dr, dc = parity_device(k)
        send_or_keep(
            i == 0, kv_send.at[dc * HEADS + lax.div(dr, 4)], kv_in.at[par, kslot], sems.at[0], sems.at[1], dr, dc
        )

    loop(0, 64, send_kv)
    to_attention(q_send, q_in, sems.at[2], sems.at[3])
    cot_copies = halo_start(gx, gedge, ghalo, 16)

    def take_skip(s):
        pre_ref[s] = nn(split, skip_ref[s])

    loop(0, 8, take_skip)
    halo_finish(gx, ghalo, cot_copies)

    def back_conv(half):
        total = jnp.zeros((512, 128), F32)
        for t, (dr, dc) in enumerate(TAPS):
            window = gx[pl.ds(4 * half, 4), 1 - dr : 3 - dr, 1 - dc : 3 - dc].reshape(512, 128)
            total = total + nn(window, wconv[t])
        dh_ref[pl.ds(4 * half, 4)] = total.reshape(4, 128, 128)

    loop(0, 2, back_conv)

    drain(kv_in.at[par], sems.at[1])
    mate_kv = remote(kv_in.at[par], kv_in.at[par], sems.at[4], sems.at[5], mate, c)
    mate_kv.start()
    drain(q_in, sems.at[3])
    for _ in range(3):
        drain(kv_send.at[pl.ds(0, 21)], sems.at[0])
    drain32(q_send, sems.at[2])
    mate_kv.wait()

    def ones_values(i):
        part = kv_in[lax.div(i, 4), pl.ds(lax.rem(i, 4) * 16, 16)].reshape(512, 128)
        lane = lax.broadcasted_iota(jnp.int32, (512, 128), 1)
        v1[pl.ds(pl.multiple_of(i * 512, 512), 512), :] = jnp.where(lane < 64, jnp.ones_like(part), part)

    loop(0, 8, ones_values)

    def keys(j):
        n = CHUNK // 32
        return kv_in[j * n // 64, (j * n) % 64 : (j * n) % 64 + n].reshape(CHUNK, 128)

    lane = lax.broadcasted_iota(jnp.int32, (BLOCK, 128), 1)

    def forward(b):
        q = q_in[pl.ds(8 * b, 8)].reshape(BLOCK, 128)
        top = None
        for j in range(4096 // CHUNK):
            s = nt(q, keys(j))
            s_ref[:, CHUNK * j : CHUNK * (j + 1)] = s
            for g in range(CHUNK // 128):
                part = s[:, 128 * g : 128 * (g + 1)]
                top = part if top is None else jnp.maximum(top, part)
        m = jnp.max(top, axis=1, keepdims=True)
        acc = jnp.zeros((BLOCK, 128), F32)
        rows = pl.ds(pl.multiple_of(b * BLOCK, BLOCK), BLOCK)
        for j in range(4096 // CHUNK):
            p = jnp.exp(s_ref[:, CHUNK * j : CHUNK * (j + 1)] - m).astype(BF)
            p_ref[rows, CHUNK * j : CHUNK * (j + 1)] = p
            acc = acc + nn(p, v1[CHUNK * j : CHUNK * (j + 1), :])
        inv = 1.0 / jnp.where(lane < 64, 1.0, pltpu.roll(acc, 64, axis=1))
        invl_ref[rows, :] = inv
        o = jnp.where(lane < 64, 0.0, acc * inv).astype(BF)
        o_buf[pl.ds(8 * b, 8)] = o.reshape(8, 32, 128)
        to_cells(o_buf, ocell, sems.at[6], sems.at[7], b)

    loop(0, 1024 // BLOCK, forward)

    levels = fscale.shape[0]
    pick = (noise_col[...] == lax.broadcasted_iota(jnp.int32, (8, levels), 1)).astype(F32)
    exact = lax.Precision.HIGHEST
    scale_rows = 1.0 + jnp.dot(pick, fscale[...], precision=exact, preferred_element_type=F32)
    shift_rows = jnp.dot(pick, fshift[...], precision=exact, preferred_element_type=F32)
    drain(ocell, sems.at[7])
    drain32(o_buf, sems.at[6])
    oc = ocell[...].reshape(8, HEADS, 32, 128)
    branch = xt.astype(F32)
    for h in range(HEADS):
        branch = branch + nt(oc[:, h].reshape(256, 128), woutn[:, 128 * h : 128 * (h + 1)])
    y = branch.astype(BF)
    y_ref[...] = y
    lifted = nt(y, wup[...])
    for s in range(8):
        u = lifted[32 * s : 32 * (s + 1)]
        pre = pre_ref[s] + jnp.concatenate([u, u, u, u], axis=0)
        pre_ref[s] = pre
        act = pre * scale_rows[s : s + 1] + shift_rows[s : s + 1]
        act_ref[s] = act
        low = (act * jax.nn.sigmoid(act)).astype(BF)
        hx[s, 1:3, 1:3] = low.reshape(2, 2, 32, 128)
        wide = low.astype(F32)
        for a in range(2):
            hedge[0, a, s : s + 1, :] = wide[64 * a : 64 * a + 1]
            hedge[1, a, s : s + 1, :] = wide[64 * a + 63 : 64 * a + 64]
    hid_copies = halo_start(hx, hedge, hhalo, 32)

    scale_terms, shift_terms = [], []
    for s in range(8):
        act = act_ref[s]
        sg = jax.nn.sigmoid(act)
        dact = dh_ref[s] * (sg * (1.0 + act * (1.0 - sg)))
        scale_terms.append(jnp.sum(dact * pre_ref[s], axis=0, keepdims=True))
        shift_terms.append(jnp.sum(dact, axis=0, keepdims=True))
        dpre = dact * scale_rows[s : s + 1]
        dh_ref[s] = dpre
        du_ref[32 * s : 32 * (s + 1)] = dpre[0:32] + dpre[32:64] + dpre[64:96] + dpre[96:128]
    du = du_ref[...].astype(BF)
    dy = nn(du, wup[...])
    dy_ref[...] = dy
    low_dy = dy.astype(BF)
    for h in range(HEADS):
        do = nn(low_dy, woutn[:, 128 * h : 128 * (h + 1)]).astype(BF).reshape(8, 32, 128)
        for s in range(8):
            do_send[s * HEADS + h] = do[s]
    to_attention(do_send, do_in, sems.at[8], sems.at[9])

    spread = (noise_row[...] == lax.broadcasted_iota(jnp.int32, (32, 8), 0)).astype(F32)
    early.put(120, jnp.dot(spread, jnp.concatenate(scale_terms, axis=0), precision=exact, preferred_element_type=F32))
    early.put(122, jnp.dot(spread, jnp.concatenate(shift_terms, axis=0), precision=exact, preferred_element_type=F32))
    grad_up = nn(du_ref[...].T.astype(BF), y)
    early.put(72, grad_up[:, 0:128])
    early.put(80, grad_up[:, 128:256])
    dyt = dy.T.astype(BF)
    wide_lane = lax.broadcasted_iota(jnp.int32, (256, 128), 1)
    for g in range(2):
        first = nn(dyt, oc[:, 2 * g].reshape(256, 128))
        second = nn(dyt, oc[:, 2 * g + 1].reshape(256, 128))
        early.put(88 + 16 * g, jnp.where(wide_lane < 64, pltpu.roll(first, 64, axis=1), second))

    halo_finish(hx, hhalo, hid_copies)

    def conv(half):
        total = jnp.zeros((512, 128), F32)
        grads = [gt[4 * half + i] for i in range(4)]
        for t, (dr, dc) in enumerate(TAPS):
            window = hx[pl.ds(4 * half, 4), 1 + dr : 3 + dr, 1 + dc : 3 + dc]
            total = total + nt(window.reshape(512, 128), wconv[t])
            term = None
            for i in range(4):
                one = nn(grads[i], window[i].reshape(128, 128))
                term = one if term is None else term + one
            gacc[t] = jnp.where(half == 0, term, gacc[t] + term)
        low = total.astype(BF)
        for i in range(4):
            dec_ref[4 * half + i] = nn(merge, low[128 * i : 128 * (i + 1)]).astype(BF)
            gskip_ref[4 * half + i] = nn(merge, dh_ref[4 * half + i].astype(BF)).astype(BF)

    gacc[...] = jnp.zeros((9, 128, 128), F32)
    loop(0, 2, conv)
    for t in range(9):
        early.put(8 * t, gacc[t])
    for k in range(124, 128):
        eg[1, k - 64] = jnp.zeros((16, 128), BF)
    early.start()

    dkvt[...] = jnp.zeros((128, 4096), F32)
    drain(do_in, sems.at[9])
    drain32(do_send, sems.at[8])
    early.scatter()

    def backward(b):
        rows = pl.ds(pl.multiple_of(b * BLOCK, BLOCK), BLOCK)
        q = q_in[pl.ds(8 * b, 8)].reshape(BLOCK, 128)
        o = o_buf[pl.ds(8 * b, 8)].reshape(BLOCK, 128).astype(F32)
        do = (do_in[pl.ds(8 * b, 8)].reshape(BLOCK, 128).astype(F32) * invl_ref[rows, :]).astype(BF)
        dof = do.astype(F32)
        delta = -jnp.sum(dof * o, axis=1, keepdims=True)
        high = delta.astype(BF).astype(F32)
        mid = (delta - high).astype(BF).astype(F32)
        rest = delta - high - mid
        ext = jnp.where(lane == 0, high, jnp.where(lane == 1, mid, jnp.where(lane == 2, rest, dof))).astype(BF)
        qt = q.astype(F32).T.astype(BF)
        dot = dof.T.astype(BF)
        dq = jnp.zeros((BLOCK, 128), F32)
        for j in range(4096 // CHUNK):
            cols = slice(CHUNK * j, CHUNK * (j + 1))
            t = nt(ext, v1[cols, :])
            p = p_ref[rows, cols]
            ds = (p.astype(F32) * t).astype(BF)
            dq = dq + nn(ds, keys(j))
            dkvt[:, cols] += nn(qt, ds) + nn(dot, p)
        dq_buf[pl.ds(8 * b, 8)] = dq.astype(BF).reshape(8, 32, 128)
        to_cells(dq_buf, dq_in, sems.at[10], sems.at[11], b)

    loop(0, 2, backward)
    early.gather()
    loop(2, 4, backward)
    early.swap()

    def give(i):
        at = pl.multiple_of((1 - par) * 2048 + i * 512, 512)
        pair_send[pl.ds(16 * i, 16)] = dkvt[:, pl.ds(at, 512)].T.astype(BF).reshape(16, 32, 128)

    loop(0, 4, give)
    swap = remote(pair_send, pair_in, sems.at[12], sems.at[13], mate, c)
    swap.start()
    swap.wait()

    def add(i):
        at = pl.multiple_of(par * 2048 + i * 512, 512)
        mine = dkvt[:, pl.ds(at, 512)].T.reshape(16, 32, 128)
        dkv_send[pl.ds(16 * i, 16)] = (mine + pair_in[pl.ds(16 * i, 16)].astype(F32)).astype(BF)

    loop(0, 4, add)
    zhi = lax.rem(lax.div(r, 2), 2)

    def send_dkv(i):
        k = lax.rem(kslot + i, 64)
        dr, dc = parity_device(k)
        send_or_keep(i == 0, dkv_send.at[k], dkv_in.at[zhi, pair_index], sems.at[14], sems.at[15], dr, dc)

    loop(0, 64, send_dkv)

    early.finish()
    for t in range(9):
        gconv_ref[t] = early.get(8 * t, 8)
    gup_ref[:, 0:128] = early.get(72, 8)
    gup_ref[:, 128:256] = early.get(80, 8)
    gout_ref[:, 0:128] = early.get(88, 16)
    gout_ref[:, 128:256] = early.get(104, 16)
    gscale_ref[...] = early.get(120, 2)[0:levels]
    gshift_ref[...] = early.get(122, 2)[0:levels]

    drain(dq_in, sems.at[11])
    drain32(dq_buf, sems.at[10])
    drain(dkv_in, sems.at[15])
    drain(dkv_send.at[pl.ds(0, 63)], sems.at[14])

    dq_all = dq_in[...].reshape(8, HEADS, 32, 128)
    dkv_all = (dkv_in[0].astype(F32) + dkv_in[1].astype(F32)).astype(BF).reshape(8, HEADS, 32, 128)
    for h in range(HEADS):
        dqt = dq_all[:, h].reshape(256, 128).astype(F32).T.astype(BF)
        dkt = dkv_all[:, h].reshape(256, 128).astype(F32).T.astype(BF)
        gq = nn(dqt, xt)[0:64] * 0.125
        gkv = nn(dkt, xt)
        for g in range(2):
            lanes = slice(128 * g, 128 * (g + 1))
            late.put(48 * g + 4 * h, gq[:, lanes])
            late.put(48 * g + 16 + 4 * h, gkv[0:64, lanes])
            late.put(48 * g + 32 + 4 * h, gkv[64:128, lanes])
    late.start()
    grad = dy_ref[...]
    for h in range(HEADS):
        rows = slice(128 * h, 128 * h + 128)
        grad = grad + nn(dq_all[:, h].reshape(256, 128), wq[rows, :])
        grad = grad + nn(dkv_all[:, h].reshape(256, 128), wkv[rows, :])
    gb_ref[...] = grad.reshape(8, 32, 256)
    late.scatter()
    late.gather()
    late.swap()
    late.finish()
    gqkv_ref[:, 0:128] = late.get(0, 48)
    gqkv_ref[:, 128:256] = late.get(48, 48)


def on_device(
    bottleneck, skip_field, cotangent, noise_level, qkv_weight, out_weight, up_weight, conv_weight,
    film_scale, film_shift,
):
    levels = film_scale.shape[0]
    x = jnp.transpose(bottleneck, (0, 2, 3, 1)).reshape(8, 32, 256)
    skip = jnp.transpose(skip_field, (0, 2, 3, 1)).reshape(8, 128, 128)
    cot = jnp.transpose(cotangent, (0, 2, 3, 1)).reshape(8, 128, 128)
    woutn = jnp.pad(out_weight.reshape(256, HEADS, 64), ((0, 0), (0, 0), (64, 0))).reshape(256, 512)

    def shape(*dims, kind=F32):
        return jax.ShapeDtypeStruct(dims, kind)

    def bf(*dims):
        return pltpu.VMEM(dims, BF)

    def f32(*dims):
        return pltpu.VMEM(dims, F32)

    packet = (32, 32, 128)
    outs = pl.pallas_call(
        kernel,
        out_shape=(
            shape(8, 128, 128, kind=BF), shape(8, 32, 256), shape(8, 128, 128, kind=BF), shape(768, 256),
            shape(256, 256), shape(128, 256), shape(9, 128, 128), shape(levels, 128), shape(levels, 128),
        ),
        in_specs=[VMEM] * 11,
        out_specs=(VMEM,) * 9,
        scratch_shapes=[
            bf(512, 256), bf(512, 256), bf(*packet), bf(*packet), bf(2, 64, 32, 128), bf(*packet),
            bf(4096, 128), f32(BLOCK, 4096), bf(1024, 4096), f32(1024, 128), bf(*packet), bf(*packet),
            bf(8, 4, 4, 32, 128), bf(8, 4, 4, 32, 128), bf(8, 128, 128),
            f32(2, 2, 8, 128), f32(2, 2, 8, 128), f32(2, 3, 2, 8, 128), f32(2, 3, 2, 8, 128),
            f32(8, 128, 128), f32(8, 128, 128), f32(8, 128, 128), bf(256, 256), f32(256, 256), f32(256, 128),
            bf(*packet), bf(*packet), f32(128, 4096), bf(*packet), bf(*packet),
            bf(64, 32, 128), bf(64, 32, 128), bf(64, 32, 128), bf(2, 32, 32, 128), f32(9, 128, 128),
            bf(2, 64, 16, 128), bf(64, 16, 128), bf(64, 16, 128), bf(64, 16, 128), bf(2, 64, 16, 128),
            bf(2, 48, 16, 128), bf(48, 16, 128), bf(48, 16, 128), bf(64, 16, 128), bf(2, 48, 16, 128),
            pltpu.SemaphoreType.DMA((64,)),
        ],
        compiler_params=pltpu.CompilerParams(
            collective_id=0, has_side_effects=True, vmem_limit_bytes=60 * 1024 * 1024
        ),
        name="unet_step",
    )(
        x, skip, cot, noise_level.reshape(8, 1), noise_level.reshape(1, 8), qkv_weight, woutn, up_weight,
        conv_weight, film_scale, film_shift,
    )
    decoded, grad_x, grad_skip = outs[:3]
    return (
        jnp.transpose(decoded.reshape(8, 2, 64, 128), (0, 3, 1, 2)),
        jnp.transpose(grad_x.reshape(8, 1, 32, 256), (0, 3, 1, 2)),
        jnp.transpose(grad_skip.reshape(8, 2, 64, 128), (0, 3, 1, 2)),
    ) + tuple(outs[3:])


def solution(mesh):
    cells = P(None, None, "rows", "cols")
    return jax.shard_map(
        on_device,
        mesh=mesh,
        in_specs=(cells, cells, cells) + (P(),) * 7,
        out_specs=(cells, cells, cells) + (P(),) * 6,
        check_vma=False,
    )
```

```python
import functools

import jax
import jax.numpy as jnp
from jax import lax
from jax.experimental import pallas as pl
from jax.experimental.pallas import tpu as pltpu
from jax.sharding import PartitionSpec as P

MESH = pl.DeviceIdType.MESH
BF = jnp.bfloat16
F32 = jnp.float32
ROWS, COLS = 16, 8
HEADS = 4
BLOCK = 256
CHUNK = 1024
TAPS = [(-1, -1), (-1, 0), (-1, 1), (0, -1), (0, 0), (0, 1), (1, -1), (1, 0), (1, 1)]
VMEM = pl.BlockSpec(memory_space=pltpu.VMEM)


def nn(a, b):
    return lax.dot_general(a, b, (((1,), (0,)), ((), ())), preferred_element_type=F32)


def nt(a, b):
    return lax.dot_general(a, b, (((1,), (1,)), ((), ())), preferred_element_type=F32)


def remote(src, dst, send, recv, row, col):
    return pltpu.make_async_remote_copy(
        src_ref=src, dst_ref=dst, send_sem=send, recv_sem=recv, device_id=(row, col), device_id_type=MESH
    )


def send_or_keep(here, src, dst, send, recv, row, col):
    @pl.when(here)
    def _():
        pltpu.make_async_copy(src, dst, recv).start()

    @pl.when(jnp.logical_not(here))
    def _():
        remote(src, dst, send, recv, row, col).start()


def drain(ref, sem):
    pltpu.make_async_copy(ref, ref, sem).wait()


def loop(lo, hi, body):
    def step(i, carry):
        body(i)
        return carry

    lax.fori_loop(lo, hi, step, 0)


def kernel(
    noise, x_ref, skip_ref, cot_ref, wqkv, wout, wup, wconv, fscale, fshift,
    dec_ref, gb_ref, gskip_ref, eag, lag,
    woutn, wq, wkv, kv_send, q_send, kv_in, q_fold, q_in, v1, xall, s_ref, p_ref, invl_ref, o_buf, o_send, o_fold,
    ocell, gx, hx, gt, gedge, hedge, ghalo, hhalo, pre_ref, act_ref, dh_ref, dy_ref, du_ref,
    do_send, do_fold, ext_ref, qt_ref, dot_ref, dkvt, dq_acc, dq_send, dq_fold, dq_in, pair_send, pair_in, dkv_send,
    dkv_in, gacc, gkv, eg, epin, ehs, ersin, lg, lrs, sems,
):
    r, c = lax.axis_index("rows"), lax.axis_index("cols")
    par = lax.rem(r, 2)
    mate = r + 1 - 2 * par
    pair = lax.div(r, 2)
    kslot = pair * COLS + c
    head, quarter = lax.div(r, 4), lax.rem(r, 4)
    qslot = quarter * COLS + c
    own = head == quarter
    spot = c * HEADS + head
    cols = [lax.rem(c + j, COLS) for j in range(COLS)]

    barrier = pltpu.get_barrier_semaphore()

    def signal(row, dc):
        pl.semaphore_signal(barrier, inc=1, device_id=(row, dc), device_id_type=MESH)

    for j in range(1, COLS):
        signal(r, cols[j])

    def signal_row(i):
        row = lax.rem(r + i, ROWS)
        for j in range(COLS):
            signal(row, cols[j])

    loop(1, ROWS, signal_row)

    def to_attention(src, dst, send, recv):
        def row(i):
            h = lax.rem(head + i, HEADS)
            dr = HEADS * h + head
            send_or_keep((i == 0) & own, src.at[c * HEADS + h], dst.at[qslot], send, recv, dr, c)
            for j in range(1, COLS):
                remote(src.at[cols[j] * HEADS + h], dst.at[qslot], send, recv, dr, cols[j]).start()

        loop(0, HEADS, row)

    def to_cells(src, dst, send, recv, row):
        dr = 4 * quarter + row
        send_or_keep(dr == r, src.at[row * COLS + c], dst.at[spot], send, recv, dr, c)
        for j in range(1, COLS):
            remote(src.at[row * COLS + cols[j]], dst.at[spot], send, recv, dr, cols[j]).start()

    def drain32(ref, sem):
        @pl.when(own)
        def _():
            drain(ref.at[pl.ds(0, 31)], sem)

        @pl.when(jnp.logical_not(own))
        def _():
            drain(ref, sem)

    def to_parity(lo, hi, source, target, send, recv, first=0, last=COLS):
        def row(i):
            at = lax.rem(pair + i, 8)
            dr = 2 * at + par
            for j in range(first, last):
                src = source(at, cols[j])
                if j == 0:
                    send_or_keep(i == 0, src, target, send, recv, dr, c)
                else:
                    remote(src, target, send, recv, dr, cols[j]).start()

        loop(lo, hi, row)

    def halo_start(ext, edge, halo, base):
        up, down = lax.rem(r + ROWS - 1, ROWS), lax.rem(r + 1, ROWS)
        left, right = cols[COLS - 1], cols[1]
        copies = [
            remote(ext.at[:, 1, pl.ds(1, 2)], ext.at[:, 3, pl.ds(1, 2)], sems.at[base], sems.at[base + 1], up, c),
            remote(ext.at[:, 2, pl.ds(1, 2)], ext.at[:, 0, pl.ds(1, 2)], sems.at[base + 2], sems.at[base + 3], down, c),
        ]
        at = base + 4
        for row, slot in ((up, 2), (r, 1), (down, 0)):
            copies.append(remote(edge.at[0], halo.at[1, slot], sems.at[at], sems.at[at + 1], row, left))
            copies.append(remote(edge.at[1], halo.at[0, slot], sems.at[at + 2], sems.at[at + 3], row, right))
            at += 4
        for copy in copies:
            copy.start()
        return copies

    def halo_finish(ext, halo, copies):
        for copy in copies:
            copy.wait()

        @pl.when(r == 0)
        def _():
            ext[:, 0, 1:3] = jnp.zeros((8, 2, 32, 128), BF)
            halo[:, 0] = jnp.zeros((2, 2, 8, 128), F32)

        @pl.when(r == ROWS - 1)
        def _():
            ext[:, 3, 1:3] = jnp.zeros((8, 2, 32, 128), BF)
            halo[:, 2] = jnp.zeros((2, 2, 8, 128), F32)

        @pl.when(c == 0)
        def _():
            halo[0] = jnp.zeros((3, 2, 8, 128), F32)

        @pl.when(c == COLS - 1)
        def _():
            halo[1] = jnp.zeros((3, 2, 8, 128), F32)

        place = lax.broadcasted_iota(jnp.int32, (32, 128), 0)

        def one(s):
            for row, (slot, a) in enumerate(((0, 1), (1, 0), (1, 1), (2, 0))):
                odd = ext[s, row, 2].astype(F32)
                even = ext[s, row, 1].astype(F32)
                before = halo[0, slot, a, pl.ds(s, 1), :]
                after = halo[1, slot, a, pl.ds(s, 1), :]
                ext[s, row, 0] = jnp.where(place == 0, before, pltpu.roll(odd, 1, axis=0)).astype(BF)
                ext[s, row, 3] = jnp.where(place == 31, after, pltpu.roll(even, 31, axis=0)).astype(BF)

        loop(0, 8, one)

    esem = [sems.at[48 + i] for i in range(8)]

    def early_put(at, value):
        n = value.shape[0] // 16
        eg[at // 64, at % 64 : at % 64 + n] = value.astype(BF).reshape(n, 16, 128)

    def early_halves():
        return remote(eg.at[1 - par], epin, esem[0], esem[1], mate, c)

    def early_scatter():
        early_halves().wait()
        ehs[...] = (eg[par].astype(F32) + epin[...].astype(F32)).astype(BF)
        to_parity(0, 8, lambda at, dc: ehs.at[at * COLS + dc], ersin.at[kslot], esem[2], esem[3])

    def early_gather():
        drain(ersin, esem[3])
        eag[par, kslot] = jnp.sum(ersin[...].astype(F32), axis=0).astype(BF)
        mine = eag.at[par, kslot]
        for j in range(1, COLS):
            remote(mine, mine, esem[4], esem[5], r, cols[j]).start()
        def row(i):
            dr = 2 * lax.rem(pair + i, 8) + par
            for j in range(COLS):
                remote(mine, mine, esem[4], esem[5], dr, cols[j]).start()

        loop(1, 8, row)

    def early_swap():
        return remote(eag.at[par], eag.at[par], esem[6], esem[7], mate, c)

    def early_drain():
        drain(eag.at[0, pl.ds(0, 63)], esem[5])
        drain(ersin.at[pl.ds(0, 63)], esem[4])
        drain(ehs.at[pl.ds(0, 63)], esem[2])

    low_lane = lax.broadcasted_iota(jnp.int32, (BLOCK, 128), 1) < 64

    def half_turn(value):
        return pltpu.roll(value, 64, axis=1)

    def fold_low(value):
        cut = value.reshape(8, 32, 128)
        first, second = cut[:, 0:16].reshape(128, 128), cut[:, 16:32].reshape(128, 128)
        return jnp.where(low_lane[0:128], first, half_turn(second)).reshape(8, 16, 128)

    def fold_high(value):
        cut = value.reshape(8, 32, 128)
        first, second = cut[:, 0:16].reshape(128, 128), cut[:, 16:32].reshape(128, 128)
        return jnp.where(low_lane[0:128], half_turn(first), second).reshape(8, 16, 128)

    def unfold(src, dst, high, clear):
        def some(i):
            at = pl.ds(8 * i, 8)
            flat = src[at].reshape(128, 128).astype(F32)
            turned = half_turn(flat)
            first, second = (turned, flat) if high else (flat, turned)
            if clear:
                keep = jnp.logical_not(low_lane[0:128]) if high else low_lane[0:128]
                first, second = jnp.where(keep, first, 0.0), jnp.where(keep, second, 0.0)
            dst[at, 0:16] = first.astype(BF).reshape(8, 16, 128)
            dst[at, 16:32] = second.astype(BF).reshape(8, 16, 128)

        loop(0, 4, some)

    zero64 = jnp.zeros((64, 256), BF)
    for h in range(HEADS):
        wq[128 * h : 128 * h + 64] = (wqkv[64 * h : 64 * h + 64].astype(F32) * 0.125).astype(BF)
        wq[128 * h + 64 : 128 * h + 128] = zero64
        wkv[128 * h : 128 * h + 64] = wqkv[256 + 64 * h : 320 + 64 * h]
        wkv[128 * h + 64 : 128 * h + 128] = wqkv[512 + 64 * h : 576 + 64 * h]
    xt = x_ref[...].reshape(256, 256)
    for h in range(HEADS):
        rows = slice(128 * h, 128 * h + 128)
        kv = nt(xt, wkv[rows, :]).astype(BF).reshape(8, 32, 128)
        q = fold_low(nt(xt, wq[rows, :])).astype(BF)
        for s in range(8):
            kv_send[s * HEADS + h] = kv[s]
            q_send[s * HEADS + h] = q[s]

    to = lax.broadcasted_iota(jnp.int32, (128, 128), 0)
    of = lax.broadcasted_iota(jnp.int32, (128, 128), 1)
    split = (of == (lax.div(to, 64) * 64 + 2 * lax.rem(to, 32) + lax.rem(lax.div(to, 32), 2))).astype(BF)
    merge = (to == (lax.div(of, 64) * 64 + 2 * lax.rem(of, 32) + lax.rem(lax.div(of, 32), 2))).astype(BF)
    eye = (to == of).astype(BF)

    def take_cot(s):
        g = nn(split, cot_ref[s])
        low = g.astype(BF)
        gx[s, 1:3, 1:3] = low.reshape(2, 2, 32, 128)
        gt[s] = nt(eye, low).astype(BF)
        for a in range(2):
            gedge[0, a, pl.ds(s, 1), :] = g[64 * a : 64 * a + 1]
            gedge[1, a, pl.ds(s, 1), :] = g[64 * a + 63 : 64 * a + 64]

    pl.semaphore_wait(barrier, ROWS * COLS - 1)
    to_parity(
        0, 8, lambda at, dc: kv_send.at[dc * HEADS + lax.div(at, 2)], kv_in.at[par, kslot], sems.at[0], sems.at[1]
    )
    to_attention(q_send, q_fold, sems.at[2], sems.at[3])
    loop(0, 8, take_cot)
    cot_copies = halo_start(gx, gedge, ghalo, 16)

    def take_skip(s):
        pre_ref[s] = nn(split, skip_ref[s])

    loop(0, 8, take_skip)
    for g in range(2):
        block = wout[:, 128 * g : 128 * (g + 1)].astype(F32)
        woutn[:, 256 * g : 256 * g + 128] = jnp.where(low_lane, 0.0, half_turn(block)).astype(BF)
        woutn[:, 256 * g + 128 : 256 * g + 256] = jnp.where(low_lane, 0.0, block).astype(BF)
    halo_finish(gx, ghalo, cot_copies)

    def back_conv(half):
        total = jnp.zeros((512, 128), F32)
        for t, (dr, dc) in enumerate(TAPS):
            window = gx[pl.ds(4 * half, 4), 1 - dr : 3 - dr, 1 - dc : 3 - dc].reshape(512, 128)
            total = total + nn(window, wconv[t])
        dh_ref[pl.ds(4 * half, 4)] = total.reshape(4, 128, 128)

    loop(0, 2, back_conv)

    drain(kv_in.at[par], sems.at[1])
    mate_kv = remote(kv_in.at[par], kv_in.at[par], sems.at[4], sems.at[5], mate, c)
    mate_kv.start()
    drain(q_fold, sems.at[3])
    unfold(q_fold, q_in, False, True)
    for _ in range(3):
        drain(kv_send.at[pl.ds(0, 21)], sems.at[0])
    drain32(q_send, sems.at[2])

    def ones_values(half):
        def some(i):
            part = kv_in[half, pl.ds(i * 16, 16)].reshape(512, 128)
            lane = lax.broadcasted_iota(jnp.int32, (512, 128), 1)
            at = pl.multiple_of(half * 2048 + i * 512, 512)
            v1[pl.ds(at, 512), :] = jnp.where(lane < 64, jnp.ones_like(part), part)

        loop(0, 4, some)

    ones_values(par)
    mate_kv.wait()
    ones_values(1 - par)
    to_parity(0, 8, lambda at, dc: x_ref.at[dc], xall.at[par, kslot], sems.at[60], sems.at[61], 0, 4)

    def keys(j):
        n = CHUNK // 32
        return kv_in[j * n // 64, (j * n) % 64 : (j * n) % 64 + n].reshape(CHUNK, 128)

    def forward(b):
        q = q_in[pl.ds(8 * b, 8)].reshape(BLOCK, 128)
        top = None
        for j in range(4096 // CHUNK):
            s = nt(q, keys(j))
            s_ref[:, CHUNK * j : CHUNK * (j + 1)] = s
            for g in range(CHUNK // 128):
                part = s[:, 128 * g : 128 * (g + 1)]
                top = part if top is None else jnp.maximum(top, part)
        m = jnp.max(top, axis=1, keepdims=True)
        acc = jnp.zeros((BLOCK, 128), F32)
        rows = pl.ds(pl.multiple_of(b * BLOCK, BLOCK), BLOCK)
        for j in range(4096 // CHUNK):
            p = jnp.exp(s_ref[:, CHUNK * j : CHUNK * (j + 1)] - m).astype(BF)
            p_ref[rows, CHUNK * j : CHUNK * (j + 1)] = p
            acc = acc + nn(p, v1[CHUNK * j : CHUNK * (j + 1), :])
        inv = 1.0 / jnp.where(low_lane, 1.0, half_turn(acc))
        invl_ref[rows, :] = inv
        o = jnp.where(low_lane, 0.0, acc * inv)
        o_buf[rows, :] = o.astype(BF)
        o_send[pl.ds(8 * b, 8)] = fold_high(o).astype(BF)
        to_cells(o_send, o_fold, sems.at[6], sems.at[7], b)

    loop(0, 1024 // BLOCK, forward)
    to_parity(0, 8, lambda at, dc: x_ref.at[dc], xall.at[par, kslot], sems.at[60], sems.at[61], 4, 8)

    levels = fscale.shape[0]
    level = lax.broadcasted_iota(jnp.int32, (levels, 128), 0)
    scales, shifts = [], []
    for s in range(8):
        here = level == noise[s]
        scales.append(1.0 + jnp.sum(jnp.where(here, fscale[...], 0.0), axis=0, keepdims=True))
        shifts.append(jnp.sum(jnp.where(here, fshift[...], 0.0), axis=0, keepdims=True))
    drain(o_fold, sems.at[7])
    drain32(o_send, sems.at[6])
    unfold(o_fold, ocell, True, False)
    oc = ocell[...].reshape(8, HEADS, 32, 128)
    branch = xt.astype(F32)
    for h in range(HEADS):
        branch = branch + nt(oc[:, h].reshape(256, 128), woutn[:, 128 * h : 128 * (h + 1)])
    y = branch.astype(BF)
    lifted = nt(y, wup[...])
    for s in range(8):
        u = lifted[32 * s : 32 * (s + 1)]
        pre = pre_ref[s] + jnp.concatenate([u, u, u, u], axis=0)
        pre_ref[s] = pre
        act = pre * scales[s] + shifts[s]
        act_ref[s] = act
        low = (act * jax.nn.sigmoid(act)).astype(BF)
        hx[s, 1:3, 1:3] = low.reshape(2, 2, 32, 128)
        wide = low.astype(F32)
        for a in range(2):
            hedge[0, a, s : s + 1, :] = wide[64 * a : 64 * a + 1]
            hedge[1, a, s : s + 1, :] = wide[64 * a + 63 : 64 * a + 64]
    hid_copies = halo_start(hx, hedge, hhalo, 32)

    spread = lax.broadcasted_iota(jnp.int32, (32, 128), 0)
    scale_sum, shift_sum = jnp.zeros((32, 128), F32), jnp.zeros((32, 128), F32)
    for s in range(8):
        act = act_ref[s]
        sg = jax.nn.sigmoid(act)
        dact = dh_ref[s] * (sg * (1.0 + act * (1.0 - sg)))
        here = spread == noise[s]
        scale_sum += jnp.where(here, jnp.sum(dact * pre_ref[s], axis=0, keepdims=True), 0.0)
        shift_sum += jnp.where(here, jnp.sum(dact, axis=0, keepdims=True), 0.0)
        dpre = dact * scales[s]
        dh_ref[s] = dpre
        du_ref[32 * s : 32 * (s + 1)] = dpre[0:32] + dpre[32:64] + dpre[64:96] + dpre[96:128]
    du = du_ref[...].astype(BF)
    dy = nn(du, wup[...])
    dy_ref[...] = dy
    low_dy = dy.astype(BF)
    for h in range(HEADS):
        do = fold_high(nn(low_dy, woutn[:, 128 * h : 128 * (h + 1)])).astype(BF)
        for s in range(8):
            do_send[s * HEADS + h] = do[s]
    to_attention(do_send, do_fold, sems.at[8], sems.at[9])

    early_put(120, scale_sum)
    early_put(122, shift_sum)
    grad_up = nn(du_ref[...].T.astype(BF), y)
    early_put(72, grad_up[:, 0:128])
    early_put(80, grad_up[:, 128:256])
    dyt = dy.T.astype(BF)
    for g in range(2):
        first = nn(dyt, oc[:, 2 * g].reshape(256, 128))
        second = nn(dyt, oc[:, 2 * g + 1].reshape(256, 128))
        early_put(88 + 16 * g, jnp.where(low_lane, half_turn(first), second))

    halo_finish(hx, hhalo, hid_copies)

    def conv(half):
        total = jnp.zeros((512, 128), F32)
        grads = [gt[4 * half + i] for i in range(4)]
        for t, (dr, dc) in enumerate(TAPS):
            window = hx[pl.ds(4 * half, 4), 1 + dr : 3 + dr, 1 + dc : 3 + dc]
            total = total + nt(window.reshape(512, 128), wconv[t])
            term = None
            for i in range(4):
                one = nn(grads[i], window[i].reshape(128, 128))
                term = one if term is None else term + one
            gacc[t] = gacc[t] + term
        low = total.astype(BF)
        for i in range(4):
            dec_ref[4 * half + i] = nn(merge, low[128 * i : 128 * (i + 1)]).astype(BF)
            gskip_ref[4 * half + i] = nn(merge, dh_ref[4 * half + i].astype(BF)).astype(BF)

    gacc[...] = jnp.zeros((9, 128, 128), F32)
    loop(0, 2, conv)
    for t in range(9):
        early_put(8 * t, gacc[t])
    for k in range(124, 128):
        eg[1, k - 64] = jnp.zeros((16, 128), BF)
    early_halves().start()

    drain(xall.at[par], sems.at[61])
    mate_x = remote(xall.at[par], xall.at[par], sems.at[62], sems.at[63], mate, c)
    mate_x.start()
    drain(xall.at[par, pl.ds(0, 63)], sems.at[60])

    drain(do_fold, sems.at[9])
    drain32(do_send, sems.at[8])
    unfold(do_fold, ocell, True, True)
    lane = lax.broadcasted_iota(jnp.int32, (BLOCK, 128), 1)

    def prepare(b):
        rows = pl.ds(pl.multiple_of(b * BLOCK, BLOCK), BLOCK)
        q = q_in[pl.ds(8 * b, 8)].reshape(BLOCK, 128)
        do = (ocell[pl.ds(8 * b, 8)].reshape(BLOCK, 128).astype(F32) * invl_ref[rows, :]).astype(BF)
        dof = do.astype(F32)
        delta = -jnp.sum(dof * o_buf[rows, :].astype(F32), axis=1, keepdims=True)
        high = delta.astype(BF).astype(F32)
        mid = (delta - high).astype(BF).astype(F32)
        rest = delta - high - mid
        ext = jnp.where(lane == 0, high, jnp.where(lane == 1, mid, jnp.where(lane == 2, rest, dof)))
        ext_ref[rows, :] = ext.astype(BF)
        qt_ref[b] = q.astype(F32).T.astype(BF)
        dot_ref[b] = dof.T.astype(BF)
        dq_acc[rows, :] = jnp.zeros((BLOCK, 128), F32)

    loop(0, 4, prepare)
    gkv[...] = jnp.zeros((256, 256), F32)
    early_scatter()
    mate_x.wait()

    def backward(half, j):
        at = pl.multiple_of(half * 2048 + j * CHUNK, CHUNK)
        kc = kv_in[half, pl.ds(32 * j, 32)].reshape(CHUNK, 128)
        vc = v1[pl.ds(at, CHUNK), :]
        for b in range(4):
            rows = slice(BLOCK * b, BLOCK * (b + 1))
            p = p_ref[rows, pl.ds(at, CHUNK)]
            ds = (p.astype(F32) * nt(ext_ref[rows, :], vc)).astype(BF)
            dq_acc[rows, :] += nn(ds, kc)
            part = nn(qt_ref[b], ds) + nn(dot_ref[b], p)
            dkvt[...] = part if b == 0 else dkvt[...] + part
        xc = xall[half, pl.ds(32 * j, 32)].reshape(CHUNK, 256)
        gkv[0:128] += nn(dkvt[...].astype(BF), xc)
        return dkvt[...].T.reshape(32, 32, 128)

    def pair_copy(j):
        at = pl.ds(32 * j, 32)
        return remote(pair_send.at[at], pair_in.at[at], sems.at[10 + j], sems.at[12 + j], mate, c)

    def mate_chunk(j):
        pair_send[pl.ds(32 * j, 32)] = backward(1 - par, j).astype(BF)
        pair_copy(j).start()

    loop(0, 2, mate_chunk)
    early_gather()
    zhi = lax.rem(pair, 2)

    def own_chunk(j):
        part = backward(par, j)
        pair_copy(j).wait()
        at = pl.ds(32 * j, 32)
        dkv_send[at] = (part + pair_in[at].astype(F32)).astype(BF)
        target = dkv_in.at[zhi, spot]

        def row(i):
            rp = 4 * j + lax.rem(pair + i, 4)
            dr = 2 * rp + par
            send_or_keep(rp == pair, dkv_send.at[rp * COLS + c], target, sems.at[14], sems.at[15], dr, c)
            for k in range(1, COLS):
                remote(dkv_send.at[rp * COLS + cols[k]], target, sems.at[14], sems.at[15], dr, cols[k]).start()

        loop(0, 4, row)

    loop(0, 2, own_chunk)

    def give_dq(b):
        rows = pl.ds(pl.multiple_of(b * BLOCK, BLOCK), BLOCK)
        dq = dq_acc[rows, :]
        dq_send[pl.ds(8 * b, 8)] = fold_low(dq).astype(BF)
        to_cells(dq_send, dq_fold, sems.at[56], sems.at[57], b)
        xq = xall[lax.rem(b, 2), pl.ds(COLS * (2 * quarter + lax.div(b, 2)), COLS)].reshape(BLOCK, 256)
        gkv[128:256] += nn(dq.T.astype(BF), xq)

    loop(0, 4, give_dq)

    for g in range(2):
        lanes = slice(128 * g, 128 * (g + 1))
        for part, (lo, factor) in enumerate(((128, 0.125), (0, 1.0), (64, 1.0))):
            piece = (gkv[lo : lo + 64, lanes] * factor).astype(BF)
            lg[12 * g + 4 * part : 12 * g + 4 * part + 4] = piece.reshape(4, 16, 128)

    def send_lg(i):
        dr = HEADS * head + i
        send_or_keep(quarter == i, lg.at[i * COLS + c], lrs.at[qslot], sems.at[58], sems.at[59], dr, c)
        for j in range(1, COLS):
            remote(lg.at[i * COLS + cols[j]], lrs.at[qslot], sems.at[58], sems.at[59], dr, cols[j]).start()

    loop(0, 3, send_lg)
    early_drain()
    last_swap = early_swap()
    last_swap.start()

    @pl.when(quarter < 3)
    def _():
        drain(lrs, sems.at[59])
        mine = lag.at[head * 24 + qslot]
        lag[head * 24 + qslot] = jnp.sum(lrs[...].astype(F32), axis=0).astype(BF)
        for j in range(1, COLS):
            remote(mine, mine, sems.at[64], sems.at[65], r, cols[j]).start()

        def row(i):
            dr = lax.rem(r + i, ROWS)
            for j in range(COLS):
                remote(mine, mine, sems.at[64], sems.at[65], dr, cols[j]).start()

        loop(1, ROWS, row)

    drain(dq_fold, sems.at[57])
    drain32(dq_send, sems.at[56])
    unfold(dq_fold, dq_in, False, False)
    drain(dkv_in, sems.at[15])
    drain(dkv_send.at[pl.ds(0, 63)], sems.at[14])
    dq_all = dq_in[...].reshape(8, HEADS, 32, 128)
    dkv_all = (dkv_in[0].astype(F32) + dkv_in[1].astype(F32)).astype(BF).reshape(8, HEADS, 32, 128)
    grad = dy_ref[...]
    for h in range(HEADS):
        rows = slice(128 * h, 128 * h + 128)
        grad = grad + nn(dq_all[:, h].reshape(256, 128), wq[rows, :])
        grad = grad + nn(dkv_all[:, h].reshape(256, 128), wkv[rows, :])
    gb_ref[...] = grad.reshape(8, 32, 256)
    last_swap.wait()

    @pl.when(quarter < 3)
    def _():
        drain(lag.at[pl.ds(0, 95)], sems.at[65])
        drain(lg.at[pl.ds(0, 23)], sems.at[58])
        for _ in range(3):
            drain(lrs, sems.at[64])
        drain(lrs.at[pl.ds(0, 31)], sems.at[64])

    @pl.when(quarter == 3)
    def _():
        drain(lag, sems.at[65])
        drain(lg, sems.at[58])


def unpack(dec, gb, gskip, eag, lag, dec_ref, gb_ref, gskip_ref, gqkv_ref, gout_ref, gup_ref, gconv_ref, gscale_ref, gshift_ref):
    dec_ref[...] = dec[...]
    gb_ref[...] = gb[...]
    gskip_ref[...] = gskip[...]

    def early(at, n):
        return eag[at // 64, at % 64 : at % 64 + n].reshape(n * 16, 128).astype(F32)

    for t in range(9):
        gconv_ref[t] = early(8 * t, 8)
    levels = gscale_ref.shape[0]
    gscale_ref[...] = early(120, 2)[0:levels]
    gshift_ref[...] = early(122, 2)[0:levels]
    for g in range(2):
        lanes = slice(128 * g, 128 * (g + 1))
        gup_ref[:, lanes] = early(72 + 8 * g, 8)
        gout_ref[:, lanes] = early(88 + 16 * g, 16)
        for part in range(3):
            for h in range(HEADS):
                at = 24 * h + 12 * g + 4 * part
                rows = slice(256 * part + 64 * h, 256 * part + 64 * h + 64)
                gqkv_ref[rows, lanes] = lag[at : at + 4].reshape(64, 128).astype(F32)


def on_device(
    bottleneck, skip_field, cotangent, noise_level, qkv_weight, out_weight, up_weight, conv_weight,
    film_scale, film_shift,
):
    levels = film_scale.shape[0]
    x = jnp.transpose(bottleneck, (0, 2, 3, 1)).reshape(8, 32, 256)
    skip = jnp.transpose(skip_field, (0, 2, 3, 1)).reshape(8, 128, 128)
    cot = jnp.transpose(cotangent, (0, 2, 3, 1)).reshape(8, 128, 128)

    def shape(*dims, kind=F32):
        return jax.ShapeDtypeStruct(dims, kind)

    def bf(*dims):
        return pltpu.VMEM(dims, BF)

    def f32(*dims):
        return pltpu.VMEM(dims, F32)

    packet, folded = (32, 32, 128), (32, 16, 128)
    cells, packed = shape(8, 128, 128, kind=BF), shape(8, 32, 256)
    parts = pl.pallas_call(
        kernel,
        out_shape=(cells, packed, cells, shape(2, 64, 16, 128, kind=BF), shape(96, 16, 128, kind=BF)),
        in_specs=[pl.BlockSpec(memory_space=pltpu.SMEM)] + [VMEM] * 9,
        out_specs=(VMEM,) * 5,
        scratch_shapes=[
            bf(256, 512), bf(512, 256), bf(512, 256), bf(*packet), bf(*folded), bf(2, 64, 32, 128), bf(*folded),
            bf(*packet), bf(4096, 128), bf(2, 64, 32, 256), f32(BLOCK, 4096), bf(1024, 4096), f32(1024, 128),
            bf(1024, 128), bf(*folded), bf(*folded),
            bf(*packet), bf(8, 4, 4, 32, 128), bf(8, 4, 4, 32, 128), bf(8, 128, 128),
            f32(2, 2, 8, 128), f32(2, 2, 8, 128), f32(2, 3, 2, 8, 128), f32(2, 3, 2, 8, 128),
            f32(8, 128, 128), f32(8, 128, 128), f32(8, 128, 128), f32(256, 256), f32(256, 128),
            bf(*folded), bf(*folded), bf(1024, 128), bf(4, 128, 256), bf(4, 128, 256), f32(128, CHUNK),
            f32(1024, 128), bf(*folded), bf(*folded), bf(*packet),
            bf(64, 32, 128), bf(64, 32, 128), bf(64, 32, 128), bf(2, 32, 32, 128), f32(9, 128, 128), f32(256, 256),
            bf(2, 64, 16, 128), bf(64, 16, 128), bf(64, 16, 128), bf(64, 16, 128),
            bf(24, 16, 128), bf(32, 16, 128),
            pltpu.SemaphoreType.DMA((72,)),
        ],
        compiler_params=pltpu.CompilerParams(
            collective_id=0, has_side_effects=True, vmem_limit_bytes=44 * 1024 * 1024
        ),
        name="unet_step",
    )(noise_level, x, skip, cot, qkv_weight, out_weight, up_weight, conv_weight, film_scale, film_shift)
    outs = pl.pallas_call(
        unpack,
        out_shape=(
            cells, packed, cells, shape(768, 256), shape(256, 256), shape(128, 256), shape(9, 128, 128),
            shape(levels, 128), shape(levels, 128),
        ),
        in_specs=[VMEM] * 5,
        out_specs=(VMEM,) * 9,
        compiler_params=pltpu.CompilerParams(vmem_limit_bytes=16 * 1024 * 1024),
        name="unpack",
    )(*parts)
    decoded, grad_x, grad_skip = outs[:3]
    return (
        jnp.transpose(decoded.reshape(8, 2, 64, 128), (0, 3, 1, 2)),
        jnp.transpose(grad_x.reshape(8, 1, 32, 256), (0, 3, 1, 2)),
        jnp.transpose(grad_skip.reshape(8, 2, 64, 128), (0, 3, 1, 2)),
    ) + tuple(outs[3:])


def solution(mesh):
    cells = P(None, None, "rows", "cols")
    return jax.shard_map(
        on_device,
        mesh=mesh,
        in_specs=(cells, cells, cells) + (P(),) * 7,
        out_specs=(cells, cells, cells) + (P(),) * 6,
        check_vma=False,
    )
```

```python
import functools

import jax
import jax.numpy as jnp
from jax import lax
from jax.experimental import pallas as pl
from jax.experimental.pallas import tpu as pltpu
from jax.sharding import PartitionSpec as P

MESH = pl.DeviceIdType.MESH
BF = jnp.bfloat16
F32 = jnp.float32
ROWS, COLS = 16, 8
HEADS = 4
BLOCK = 256
CHUNK = 1024
TAPS = [(-1, -1), (-1, 0), (-1, 1), (0, -1), (0, 0), (0, 1), (1, -1), (1, 0), (1, 1)]
VMEM = pl.BlockSpec(memory_space=pltpu.VMEM)
ANY = pl.BlockSpec(memory_space=pltpu.HBM)


def nn(a, b):
    return lax.dot_general(a, b, (((1,), (0,)), ((), ())), preferred_element_type=F32)


def nt(a, b):
    return lax.dot_general(a, b, (((1,), (1,)), ((), ())), preferred_element_type=F32)


def remote(src, dst, send, recv, row, col):
    return pltpu.make_async_remote_copy(
        src_ref=src, dst_ref=dst, send_sem=send, recv_sem=recv, device_id=(row, col), device_id_type=MESH
    )


def send_or_keep(here, src, dst, send, recv, row, col):
    @pl.when(here)
    def _():
        pltpu.make_async_copy(src, dst, recv).start()

    @pl.when(jnp.logical_not(here))
    def _():
        remote(src, dst, send, recv, row, col).start()


def drain(ref, sem):
    pltpu.make_async_copy(ref, ref, sem).wait()


def loop(lo, hi, body):
    def step(i, carry):
        body(i)
        return carry

    lax.fori_loop(lo, hi, step, 0)


def kernel(
    noise_hbm, x_hbm, skip_hbm, cot_hbm, wqkv_hbm, wout_hbm, wup_hbm, wconv_hbm, fscale_hbm, fshift_hbm,
    dec_ref, gb_ref, gskip_ref, eag, lag,
    noise, x_ref, skip_ref, cot_ref, wqkv, wout, wup, wconv, fscale, fshift,
    woutn, wq, wkv, kv_send, q_send, kv_in, q_fold, q_in, v1, xall, s_ref, top_ref, p_ref, invl_ref, o_buf, o_send, o_fold,
    ocell, gx, hx, gt, gedge, hedge, ghalo, hhalo, pre_ref, act_ref, dh_ref, dy_ref, du_ref,
    do_send, do_fold, ext_ref, qt_ref, dot_ref, dkvt, dq_acc, dq_send, dq_fold, dq_in, pair_send, pair_in, dkv_send,
    dkv_in, gacc, gkv, eg, epin, ehs, ersin, lg, lrs, sems,
):
    r, c = lax.axis_index("rows"), lax.axis_index("cols")
    par = lax.rem(r, 2)
    mate = r + 1 - 2 * par
    pair = lax.div(r, 2)
    kslot = pair * COLS + c
    head, quarter = lax.div(r, 4), lax.rem(r, 4)
    zhi, group = lax.rem(pair, 2), lax.div(pair, 4)
    qslot = lax.rem(pair, 4) * COLS + c
    own = zhi == group
    spot = c * HEADS + head
    sign = 1 - 2 * par
    cols = [lax.rem(c + COLS + sign * j, COLS) for j in range(COLS)]

    def pair_at(i):
        return lax.rem(pair + 8 + sign * i, 8)

    loads = [
        pltpu.make_async_copy(src, dst, sems.at[104 + i])
        for i, (src, dst) in enumerate((
            (x_hbm, x_ref), (wqkv_hbm, wqkv), (cot_hbm, cot_ref), (skip_hbm, skip_ref), (wout_hbm, wout),
            (wup_hbm, wup), (wconv_hbm, wconv), (fscale_hbm, fscale), (fshift_hbm, fshift), (noise_hbm, noise),
        ))
    ]
    for load in loads:
        load.start()

    barrier = pltpu.get_barrier_semaphore()

    def signal(row, dc):
        pl.semaphore_signal(barrier, inc=1, device_id=(row, dc), device_id_type=MESH)

    for j in range(1, COLS):
        signal(r, cols[j])

    def signal_row(i):
        row = lax.rem(r + i, ROWS)
        for j in range(COLS):
            signal(row, cols[j])

    loop(1, ROWS, signal_row)

    def to_attention(src, dst, send, recv):
        def row(i):
            h = lax.rem(head + i, HEADS)
            dr = HEADS * h + 2 * group + par
            send_or_keep((i == 0) & own, src.at[c * HEADS + h], dst.at[qslot], send, recv, dr, c)
            for j in range(1, COLS):
                remote(src.at[cols[j] * HEADS + h], dst.at[qslot], send, recv, dr, cols[j]).start()

        loop(0, HEADS, row)

    def to_cells(src, dst, send, recv, row):
        dr = 2 * (4 * zhi + row) + par
        send_or_keep(dr == r, src.at[row * COLS + c], dst.at[spot], send, recv, dr, c)
        for j in range(1, COLS):
            remote(src.at[row * COLS + cols[j]], dst.at[spot], send, recv, dr, cols[j]).start()

    def drain32(ref, sem):
        @pl.when(own)
        def _():
            drain(ref.at[pl.ds(0, 31)], sem)

        @pl.when(jnp.logical_not(own))
        def _():
            drain(ref, sem)

    def to_parity(lo, hi, source, target, send, recv, first=0, last=COLS):
        def row(i):
            at = pair_at(i)
            dr = 2 * at + par
            got = recv(i) if callable(recv) else recv
            for j in range(first, last):
                src = source(at, cols[j])
                if j == 0:
                    send_or_keep(i == 0, src, target, send, got, dr, c)
                else:
                    remote(src, target, send, got, dr, cols[j]).start()

        loop(lo, hi, row)

    def halo_start(ext, edge, halo, base):
        up, down = lax.rem(r + ROWS - 1, ROWS), lax.rem(r + 1, ROWS)
        left, right = lax.rem(c + COLS - 1, COLS), lax.rem(c + 1, COLS)
        copies = [
            remote(ext.at[:, 1, pl.ds(1, 2)], ext.at[:, 3, pl.ds(1, 2)], sems.at[base], sems.at[base + 1], up, c),
            remote(ext.at[:, 2, pl.ds(1, 2)], ext.at[:, 0, pl.ds(1, 2)], sems.at[base + 2], sems.at[base + 3], down, c),
        ]
        at = base + 4
        for row, slot in ((up, 2), (r, 1), (down, 0)):
            copies.append(remote(edge.at[0], halo.at[1, slot], sems.at[at], sems.at[at + 1], row, left))
            copies.append(remote(edge.at[1], halo.at[0, slot], sems.at[at + 2], sems.at[at + 3], row, right))
            at += 4
        for copy in copies:
            copy.start()
        return copies

    def halo_finish(ext, halo, copies):
        for copy in copies:
            copy.wait()

        @pl.when(r == 0)
        def _():
            ext[:, 0, 1:3] = jnp.zeros((8, 2, 32, 128), BF)
            halo[:, 0] = jnp.zeros((2, 2, 8, 128), F32)

        @pl.when(r == ROWS - 1)
        def _():
            ext[:, 3, 1:3] = jnp.zeros((8, 2, 32, 128), BF)
            halo[:, 2] = jnp.zeros((2, 2, 8, 128), F32)

        @pl.when(c == 0)
        def _():
            halo[0] = jnp.zeros((3, 2, 8, 128), F32)

        @pl.when(c == COLS - 1)
        def _():
            halo[1] = jnp.zeros((3, 2, 8, 128), F32)

        place = lax.broadcasted_iota(jnp.int32, (32, 128), 0)

        def one(s):
            for row, (slot, a) in enumerate(((0, 1), (1, 0), (1, 1), (2, 0))):
                odd = ext[s, row, 2].astype(F32)
                even = ext[s, row, 1].astype(F32)
                before = halo[0, slot, a, pl.ds(s, 1), :]
                after = halo[1, slot, a, pl.ds(s, 1), :]
                ext[s, row, 0] = jnp.where(place == 0, before, pltpu.roll(odd, 1, axis=0)).astype(BF)
                ext[s, row, 3] = jnp.where(place == 31, after, pltpu.roll(even, 31, axis=0)).astype(BF)

        loop(0, 8, one)

    esem = [sems.at[48 + i] for i in range(8)]

    def early_put(at, value):
        n = value.shape[0] // 16
        eg[at // 64, at % 64 : at % 64 + n] = value.astype(BF).reshape(n, 16, 128)

    def early_halves():
        return remote(eg.at[1 - par], epin, esem[0], esem[1], mate, c)

    def early_scatter():
        early_halves().wait()
        ehs[...] = (eg[par].astype(F32) + epin[...].astype(F32)).astype(BF)
        to_parity(0, 8, lambda at, dc: ehs.at[at * COLS + dc], ersin.at[kslot], esem[2], esem[3])

    def early_gather():
        drain(ersin, esem[3])
        eag[par, kslot] = jnp.sum(ersin[...].astype(F32), axis=0).astype(BF)
        mine = eag.at[par, kslot]
        for j in range(1, COLS):
            remote(mine, mine, esem[4], esem[5], r, cols[j]).start()
        def row(i):
            dr = 2 * pair_at(i) + par
            for j in range(COLS):
                remote(mine, mine, esem[4], esem[5], dr, cols[j]).start()

        loop(1, 8, row)

    def early_swap():
        return remote(eag.at[par], eag.at[par], esem[6], esem[7], mate, c)

    def early_drain():
        drain(eag.at[0, pl.ds(0, 63)], esem[5])
        drain(ersin.at[pl.ds(0, 63)], esem[4])
        drain(ehs.at[pl.ds(0, 63)], esem[2])

    low_lane = lax.broadcasted_iota(jnp.int32, (BLOCK, 128), 1) < 64

    def half_turn(value):
        return pltpu.roll(value, 64, axis=1)

    def fold_low(value):
        cut = value.reshape(8, 32, 128)
        first, second = cut[:, 0:16].reshape(128, 128), cut[:, 16:32].reshape(128, 128)
        return jnp.where(low_lane[0:128], first, half_turn(second)).reshape(8, 16, 128)

    def fold_high(value):
        cut = value.reshape(8, 32, 128)
        first, second = cut[:, 0:16].reshape(128, 128), cut[:, 16:32].reshape(128, 128)
        return jnp.where(low_lane[0:128], half_turn(first), second).reshape(8, 16, 128)

    def unfold(src, dst, high, clear):
        def some(i):
            at = pl.ds(8 * i, 8)
            flat = src[at].reshape(128, 128).astype(F32)
            turned = half_turn(flat)
            first, second = (turned, flat) if high else (flat, turned)
            if clear:
                keep = jnp.logical_not(low_lane[0:128]) if high else low_lane[0:128]
                first, second = jnp.where(keep, first, 0.0), jnp.where(keep, second, 0.0)
            dst[at, 0:16] = first.astype(BF).reshape(8, 16, 128)
            dst[at, 16:32] = second.astype(BF).reshape(8, 16, 128)

        loop(0, 4, some)

    loads[0].wait()
    loads[1].wait()
    zero64 = jnp.zeros((64, 256), BF)
    for h in range(HEADS):
        wq[128 * h : 128 * h + 64] = (wqkv[64 * h : 64 * h + 64].astype(F32) * 0.125).astype(BF)
        wq[128 * h + 64 : 128 * h + 128] = zero64
        wkv[128 * h : 128 * h + 64] = wqkv[256 + 64 * h : 320 + 64 * h]
        wkv[128 * h + 64 : 128 * h + 128] = wqkv[512 + 64 * h : 576 + 64 * h]
    xt = x_ref[...].reshape(256, 256)
    for h in range(HEADS):
        rows = slice(128 * h, 128 * h + 128)
        kv = nt(xt, wkv[rows, :]).astype(BF).reshape(8, 32, 128)
        q = fold_low(nt(xt, wq[rows, :])).astype(BF)
        for s in range(8):
            kv_send[s * HEADS + h] = kv[s]
            q_send[s * HEADS + h] = q[s]

    to = lax.broadcasted_iota(jnp.int32, (128, 128), 0)
    of = lax.broadcasted_iota(jnp.int32, (128, 128), 1)
    split = (of == (lax.div(to, 64) * 64 + 2 * lax.rem(to, 32) + lax.rem(lax.div(to, 32), 2))).astype(BF)
    merge = (to == (lax.div(of, 64) * 64 + 2 * lax.rem(of, 32) + lax.rem(lax.div(of, 32), 2))).astype(BF)
    eye = (to == of).astype(BF)

    def take_cot(s):
        g = nn(split, cot_ref[s])
        low = g.astype(BF)
        gx[s, 1:3, 1:3] = low.reshape(2, 2, 32, 128)
        gt[s] = nt(eye, low).astype(BF)
        for a in range(2):
            gedge[0, a, pl.ds(s, 1), :] = g[64 * a : 64 * a + 1]
            gedge[1, a, pl.ds(s, 1), :] = g[64 * a + 63 : 64 * a + 64]

    pl.semaphore_wait(barrier, ROWS * COLS - 1)
    to_attention(q_send, q_fold, sems.at[2], sems.at[3])
    to_parity(
        0, 8, lambda at, dc: kv_send.at[dc * HEADS + lax.div(at, 2)], kv_in.at[par, kslot], sems.at[0],
        lambda i: sems.at[80 + i],
    )
    loads[2].wait()
    loop(0, 8, take_cot)
    cot_copies = halo_start(gx, gedge, ghalo, 16)
    for load in loads[3:]:
        load.wait()

    def take_skip(s):
        pre_ref[s] = nn(split, skip_ref[s])

    loop(0, 8, take_skip)
    for g in range(2):
        block = wout[:, 128 * g : 128 * (g + 1)].astype(F32)
        woutn[:, 256 * g : 256 * g + 128] = jnp.where(low_lane, 0.0, half_turn(block)).astype(BF)
        woutn[:, 256 * g + 128 : 256 * g + 256] = jnp.where(low_lane, 0.0, block).astype(BF)

    def back_conv(half):
        total = jnp.zeros((512, 128), F32)
        for t, (dr, dc) in enumerate(TAPS):
            window = gx[pl.ds(4 * half, 4), 1 - dr : 3 - dr, 1 - dc : 3 - dc].reshape(512, 128)
            total = total + nn(window, wconv[t])
        dh_ref[pl.ds(4 * half, 4)] = total.reshape(4, 128, 128)

    drain(q_fold, sems.at[3])
    unfold(q_fold, q_in, False, True)
    top_ref[...] = jnp.full((1024, 128), -jnp.inf, F32)

    def score(half, at):
        part = kv_in[half, pl.ds(COLS * at, COLS)].reshape(256, 128)
        place = pl.multiple_of(half * 2048 + at * 256, 256)
        v1[pl.ds(place, 256), :] = jnp.where(low_lane, jnp.ones_like(part), part)
        for b in range(4):
            rows = slice(BLOCK * b, BLOCK * (b + 1))
            s = nt(q_in[8 * b : 8 * b + 8].reshape(BLOCK, 128), part)
            s_ref[rows, pl.ds(place, 256)] = s
            top_ref[rows, :] = jnp.maximum(top_ref[rows, :], jnp.maximum(s[:, 0:128], s[:, 128:256]))

    def mate_group(i):
        at = kv_in.at[par, pl.ds(COLS * lax.rem(pair + 8 - sign * i, 8), COLS)]
        return remote(at, at, sems.at[88 + i], sems.at[96 + i], mate, c)

    def take_group(i):
        at = lax.rem(pair + 8 - sign * i, 8)
        drain(kv_in.at[par, pl.ds(COLS * at, COLS)], sems.at[80 + i])
        mate_group(i).start()
        score(par, at)

    def take_mate(i):
        mate_group(i).wait()
        score(1 - par, pair_at(i))

    take_group(0)

    def both(i):
        take_group(i)
        take_mate(i - 1)

    loop(1, 8, both)
    to_parity(0, 8, lambda at, dc: x_ref.at[dc], xall.at[kslot], sems.at[60], sems.at[61], 0, 4)
    take_mate(7)
    for _ in range(3):
        drain(kv_send.at[pl.ds(0, 21)], sems.at[0])
    drain32(q_send, sems.at[2])

    def forward(b):
        rows = pl.ds(pl.multiple_of(b * BLOCK, BLOCK), BLOCK)
        m = jnp.max(top_ref[rows, :], axis=1, keepdims=True)
        acc = jnp.zeros((BLOCK, 128), F32)
        for j in range(4096 // CHUNK):
            p = jnp.exp(s_ref[rows, CHUNK * j : CHUNK * (j + 1)] - m).astype(BF)
            p_ref[rows, CHUNK * j : CHUNK * (j + 1)] = p
            acc = acc + nn(p, v1[CHUNK * j : CHUNK * (j + 1), :])
        inv = 1.0 / jnp.where(low_lane, 1.0, half_turn(acc))
        invl_ref[rows, :] = inv
        o = jnp.where(low_lane, 0.0, acc * inv)
        o_buf[rows, :] = o.astype(BF)
        o_send[pl.ds(8 * b, 8)] = fold_high(o).astype(BF)
        to_cells(o_send, o_fold, sems.at[6], sems.at[7], b)

    loop(0, 1024 // BLOCK, forward)
    halo_finish(gx, ghalo, cot_copies)
    loop(0, 2, back_conv)

    levels = fscale.shape[0]
    level = lax.broadcasted_iota(jnp.int32, (levels, 128), 0)
    scales, shifts = [], []
    for s in range(8):
        here = level == noise[s]
        scales.append(1.0 + jnp.sum(jnp.where(here, fscale[...], 0.0), axis=0, keepdims=True))
        shifts.append(jnp.sum(jnp.where(here, fshift[...], 0.0), axis=0, keepdims=True))
    drain(o_fold, sems.at[7])
    drain32(o_send, sems.at[6])
    unfold(o_fold, ocell, True, False)
    oc = ocell[...].reshape(8, HEADS, 32, 128)
    branch = x_ref[...].reshape(256, 256).astype(F32)
    for h in range(HEADS):
        branch = branch + nt(oc[:, h].reshape(256, 128), woutn[:, 128 * h : 128 * (h + 1)])
    y = branch.astype(BF)
    lifted = nt(y, wup[...])
    for s in range(8):
        u = lifted[32 * s : 32 * (s + 1)]
        pre = pre_ref[s] + jnp.concatenate([u, u, u, u], axis=0)
        pre_ref[s] = pre
        act = pre * scales[s] + shifts[s]
        act_ref[s] = act
        low = (act * jax.nn.sigmoid(act)).astype(BF)
        hx[s, 1:3, 1:3] = low.reshape(2, 2, 32, 128)
        wide = low.astype(F32)
        for a in range(2):
            hedge[0, a, s : s + 1, :] = wide[64 * a : 64 * a + 1]
            hedge[1, a, s : s + 1, :] = wide[64 * a + 63 : 64 * a + 64]
    hid_copies = halo_start(hx, hedge, hhalo, 32)

    spread = lax.broadcasted_iota(jnp.int32, (32, 128), 0)
    scale_sum, shift_sum = jnp.zeros((32, 128), F32), jnp.zeros((32, 128), F32)
    for s in range(8):
        act = act_ref[s]
        sg = jax.nn.sigmoid(act)
        dact = dh_ref[s] * (sg * (1.0 + act * (1.0 - sg)))
        here = spread == noise[s]
        scale_sum += jnp.where(here, jnp.sum(dact * pre_ref[s], axis=0, keepdims=True), 0.0)
        shift_sum += jnp.where(here, jnp.sum(dact, axis=0, keepdims=True), 0.0)
        dpre = dact * scales[s]
        dh_ref[s] = dpre
        du_ref[32 * s : 32 * (s + 1)] = dpre[0:32] + dpre[32:64] + dpre[64:96] + dpre[96:128]
    du = du_ref[...].astype(BF)
    dy = nn(du, wup[...])
    dy_ref[...] = dy
    low_dy = dy.astype(BF)
    for h in range(HEADS):
        do = fold_high(nn(low_dy, woutn[:, 128 * h : 128 * (h + 1)])).astype(BF)
        for s in range(8):
            do_send[s * HEADS + h] = do[s]
    to_attention(do_send, do_fold, sems.at[8], sems.at[9])
    to_parity(0, 8, lambda at, dc: x_ref.at[dc], xall.at[kslot], sems.at[60], sems.at[61], 4, 8)

    early_put(120, scale_sum)
    early_put(122, shift_sum)
    grad_up = nn(du_ref[...].T.astype(BF), y)
    early_put(72, grad_up[:, 0:128])
    early_put(80, grad_up[:, 128:256])
    dyt = dy.T.astype(BF)
    for g in range(2):
        first = nn(dyt, oc[:, 2 * g].reshape(256, 128))
        second = nn(dyt, oc[:, 2 * g + 1].reshape(256, 128))
        early_put(88 + 16 * g, jnp.where(low_lane, half_turn(first), second))

    halo_finish(hx, hhalo, hid_copies)

    def conv(half):
        total = jnp.zeros((512, 128), F32)
        grads = [gt[4 * half + i] for i in range(4)]
        for t, (dr, dc) in enumerate(TAPS):
            window = hx[pl.ds(4 * half, 4), 1 + dr : 3 + dr, 1 + dc : 3 + dc]
            total = total + nt(window.reshape(512, 128), wconv[t])
            term = None
            for i in range(4):
                one = nn(grads[i], window[i].reshape(128, 128))
                term = one if term is None else term + one
            gacc[t] = gacc[t] + term
        low = total.astype(BF)
        for i in range(4):
            dec_ref[4 * half + i] = nn(merge, low[128 * i : 128 * (i + 1)]).astype(BF)
            gskip_ref[4 * half + i] = nn(merge, dh_ref[4 * half + i].astype(BF)).astype(BF)

    gacc[...] = jnp.zeros((9, 128, 128), F32)
    loop(0, 2, conv)
    for t in range(9):
        early_put(8 * t, gacc[t])
    for k in range(124, 128):
        eg[1, k - 64] = jnp.zeros((16, 128), BF)
    early_halves().start()

    drain(do_fold, sems.at[9])
    drain32(do_send, sems.at[8])
    unfold(do_fold, ocell, True, True)
    lane = lax.broadcasted_iota(jnp.int32, (BLOCK, 128), 1)

    def prepare(b):
        rows = pl.ds(pl.multiple_of(b * BLOCK, BLOCK), BLOCK)
        q = q_in[pl.ds(8 * b, 8)].reshape(BLOCK, 128)
        do = (ocell[pl.ds(8 * b, 8)].reshape(BLOCK, 128).astype(F32) * invl_ref[rows, :]).astype(BF)
        dof = do.astype(F32)
        delta = -jnp.sum(dof * o_buf[rows, :].astype(F32), axis=1, keepdims=True)
        high = delta.astype(BF).astype(F32)
        mid = (delta - high).astype(BF).astype(F32)
        rest = delta - high - mid
        ext = jnp.where(lane == 0, high, jnp.where(lane == 1, mid, jnp.where(lane == 2, rest, dof)))
        ext_ref[rows, :] = ext.astype(BF)
        qt_ref[b] = q.astype(F32).T.astype(BF)
        dot_ref[b] = dof.T.astype(BF)
        dq_acc[rows, :] = jnp.zeros((BLOCK, 128), F32)

    loop(0, 4, prepare)
    gkv[...] = jnp.zeros((256, 256), F32)
    early_scatter()

    def backward(half, j):
        at = pl.multiple_of(half * 2048 + j * CHUNK, CHUNK)
        kc = kv_in[half, pl.ds(32 * j, 32)].reshape(CHUNK, 128)
        vc = v1[pl.ds(at, CHUNK), :]
        for b in range(4):
            rows = slice(BLOCK * b, BLOCK * (b + 1))
            p = p_ref[rows, pl.ds(at, CHUNK)]
            ds = (p.astype(F32) * nt(ext_ref[rows, :], vc)).astype(BF)
            dq_acc[rows, :] += nn(ds, kc)
            part = nn(qt_ref[b], ds) + nn(dot_ref[b], p)
            dkvt[...] = part if b == 0 else dkvt[...] + part

    def pair_copy(j):
        return remote(pair_send.at[j], pair_in.at[j], sems.at[10 + j], sems.at[12 + j], mate, c)

    def mate_chunk(j):
        backward(1 - par, j)
        pair_send[j] = dkvt[...].astype(BF)
        pair_copy(j).start()

    loop(0, 2, mate_chunk)
    early_gather()
    drain(xall, sems.at[61])
    drain(xall.at[pl.ds(0, 63)], sems.at[60])

    def own_chunk(j):
        backward(par, j)
        pair_copy(j).wait()
        total = dkvt[...] + pair_in[j].astype(F32)
        dkv_send[pl.ds(32 * j, 32)] = total.T.astype(BF).reshape(32, 32, 128)
        target = dkv_in.at[zhi, spot]

        def row(i):
            rp = 4 * j + lax.rem(pair + i, 4)
            dr = 2 * rp + par
            send_or_keep(rp == pair, dkv_send.at[rp * COLS + c], target, sems.at[14], sems.at[15], dr, c)
            for k in range(1, COLS):
                remote(dkv_send.at[rp * COLS + cols[k]], target, sems.at[14], sems.at[15], dr, cols[k]).start()

        loop(0, 4, row)
        gkv[0:128] += nn(total.astype(BF), xall[pl.ds(32 * j, 32)].reshape(CHUNK, 256))

    loop(0, 2, own_chunk)

    def give_dq(b):
        rows = pl.ds(pl.multiple_of(b * BLOCK, BLOCK), BLOCK)
        dq = dq_acc[rows, :]
        dq_send[pl.ds(8 * b, 8)] = fold_low(dq).astype(BF)
        to_cells(dq_send, dq_fold, sems.at[56], sems.at[57], b)
        xq = xall[pl.ds(COLS * (4 * zhi + b), COLS)].reshape(BLOCK, 256)
        gkv[128:256] += nn(dq.T.astype(BF), xq)

    loop(0, 4, give_dq)

    for g in range(2):
        lanes = slice(128 * g, 128 * (g + 1))
        for part, (lo, factor) in enumerate(((128, 0.125), (0, 1.0), (64, 1.0))):
            piece = (gkv[lo : lo + 64, lanes] * factor).astype(BF)
            lg[12 * g + 4 * part : 12 * g + 4 * part + 4] = piece.reshape(4, 16, 128)

    member = quarter * COLS + c

    def send_lg(i):
        dr = HEADS * head + i
        send_or_keep(quarter == i, lg.at[i * COLS + c], lrs.at[member], sems.at[58], sems.at[59], dr, c)
        for j in range(1, COLS):
            remote(lg.at[i * COLS + cols[j]], lrs.at[member], sems.at[58], sems.at[59], dr, cols[j]).start()

    loop(0, 3, send_lg)
    early_drain()
    last_swap = early_swap()
    last_swap.start()

    @pl.when(quarter < 3)
    def _():
        drain(lrs, sems.at[59])
        mine = lag.at[head * 24 + member]
        lag[head * 24 + member] = jnp.sum(lrs[...].astype(F32), axis=0).astype(BF)
        for j in range(1, COLS):
            remote(mine, mine, sems.at[64], sems.at[65], r, cols[j]).start()

        def row(i):
            dr = lax.rem(r + i, ROWS)
            for j in range(COLS):
                remote(mine, mine, sems.at[64], sems.at[65], dr, cols[j]).start()

        loop(1, ROWS, row)

    drain(dq_fold, sems.at[57])
    drain32(dq_send, sems.at[56])
    unfold(dq_fold, dq_in, False, False)
    drain(dkv_in, sems.at[15])
    drain(dkv_send.at[pl.ds(0, 63)], sems.at[14])
    dq_all = dq_in[...].reshape(8, HEADS, 32, 128)
    dkv_all = (dkv_in[0].astype(F32) + dkv_in[1].astype(F32)).astype(BF).reshape(8, HEADS, 32, 128)
    grad = dy_ref[...]
    for h in range(HEADS):
        rows = slice(128 * h, 128 * h + 128)
        grad = grad + nn(dq_all[:, h].reshape(256, 128), wq[rows, :])
        grad = grad + nn(dkv_all[:, h].reshape(256, 128), wkv[rows, :])
    gb_ref[...] = grad.reshape(8, 32, 256)
    last_swap.wait()

    @pl.when(quarter < 3)
    def _():
        drain(lag.at[pl.ds(0, 95)], sems.at[65])
        drain(lg.at[pl.ds(0, 23)], sems.at[58])
        for _ in range(3):
            drain(lrs, sems.at[64])
        drain(lrs.at[pl.ds(0, 31)], sems.at[64])

    @pl.when(quarter == 3)
    def _():
        drain(lag, sems.at[65])
        drain(lg, sems.at[58])


def unpack(
    dec, gb, gskip, eag, lag, dec_ref, gb_ref, gskip_ref, gqkv_ref, gout_ref, gup_ref, gconv_ref, gscale_ref, gshift_ref,
    dec_v, gb_v, gskip_v, eag_v, lag_v, gqkv_v, gout_v, gup_v, gconv_v, gscale_v, gshift_v, sems,
):
    held = (dec_v, gb_v, gskip_v, eag_v, lag_v)
    loads = [
        pltpu.make_async_copy(src, dst, sems.at[i]) for i, (src, dst) in enumerate(zip((dec, gb, gskip, eag, lag), held))
    ]
    for load in loads:
        load.start()
    stores = [
        pltpu.make_async_copy(src, dst, sems.at[5 + i])
        for i, (src, dst) in enumerate((
            (dec_v, dec_ref), (gb_v, gb_ref), (gskip_v, gskip_ref), (gconv_v, gconv_ref), (gscale_v, gscale_ref),
            (gshift_v, gshift_ref), (gup_v, gup_ref), (gout_v, gout_ref), (gqkv_v, gqkv_ref),
        ))
    ]
    loads[3].wait()

    def early(at, n):
        return eag_v[at // 64, at % 64 : at % 64 + n].reshape(n * 16, 128).astype(F32)

    for t in range(9):
        gconv_v[t] = early(8 * t, 8)
    stores[3].start()
    levels = gscale_v.shape[0]
    gscale_v[...] = early(120, 2)[0:levels]
    gshift_v[...] = early(122, 2)[0:levels]
    for g in range(2):
        lanes = slice(128 * g, 128 * (g + 1))
        gup_v[:, lanes] = early(72 + 8 * g, 8)
        gout_v[:, lanes] = early(88 + 16 * g, 16)
    for i in range(4, 8):
        stores[i].start()
    loads[4].wait()
    for g in range(2):
        lanes = slice(128 * g, 128 * (g + 1))
        for part in range(3):
            for h in range(HEADS):
                at = 24 * h + 12 * g + 4 * part
                rows = slice(256 * part + 64 * h, 256 * part + 64 * h + 64)
                gqkv_v[rows, lanes] = lag_v[at : at + 4].reshape(64, 128).astype(F32)
    stores[8].start()
    for i in range(3):
        loads[i].wait()
        stores[i].start()
    for store in stores:
        store.wait()


def on_device(
    bottleneck, skip_field, cotangent, noise_level, qkv_weight, out_weight, up_weight, conv_weight,
    film_scale, film_shift,
):
    levels = film_scale.shape[0]
    x = jnp.transpose(bottleneck, (0, 2, 3, 1)).reshape(8, 32, 256)
    skip = jnp.transpose(skip_field, (0, 2, 3, 1)).reshape(8, 128, 128)
    cot = jnp.transpose(cotangent, (0, 2, 3, 1)).reshape(8, 128, 128)

    def shape(*dims, kind=F32):
        return jax.ShapeDtypeStruct(dims, kind)

    def bf(*dims):
        return pltpu.VMEM(dims, BF)

    def f32(*dims):
        return pltpu.VMEM(dims, F32)

    packet, folded = (32, 32, 128), (32, 16, 128)
    cells, packed = shape(8, 128, 128, kind=BF), shape(8, 32, 256)
    parts = pl.pallas_call(
        kernel,
        out_shape=(cells, packed, cells, shape(2, 64, 16, 128, kind=BF), shape(96, 16, 128, kind=BF)),
        in_specs=[ANY] * 10,
        out_specs=(VMEM,) * 5,
        scratch_shapes=[
            pltpu.SMEM((8,), jnp.int32), bf(8, 32, 256), bf(8, 128, 128), bf(8, 128, 128), bf(768, 256), bf(256, 256),
            bf(128, 256), bf(9, 128, 128), f32(levels, 128), f32(levels, 128),
            bf(256, 512), bf(512, 256), bf(512, 256), bf(*packet), bf(*folded), bf(2, 64, 32, 128), bf(*folded),
            bf(*packet), bf(4096, 128), bf(64, 32, 256), f32(1024, 4096), f32(1024, 128), bf(1024, 4096), f32(1024, 128),
            bf(1024, 128), bf(*folded), bf(*folded),
            bf(*packet), bf(8, 4, 4, 32, 128), bf(8, 4, 4, 32, 128), bf(8, 128, 128),
            f32(2, 2, 8, 128), f32(2, 2, 8, 128), f32(2, 3, 2, 8, 128), f32(2, 3, 2, 8, 128),
            f32(8, 128, 128), f32(8, 128, 128), f32(8, 128, 128), f32(256, 256), f32(256, 128),
            bf(*folded), bf(*folded), bf(1024, 128), bf(4, 128, 256), bf(4, 128, 256), f32(128, CHUNK),
            f32(1024, 128), bf(*folded), bf(*folded), bf(*packet),
            bf(2, 128, CHUNK), bf(2, 128, CHUNK), bf(64, 32, 128), bf(2, 32, 32, 128), f32(9, 128, 128), f32(256, 256),
            bf(2, 64, 16, 128), bf(64, 16, 128), bf(64, 16, 128), bf(64, 16, 128),
            bf(24, 16, 128), bf(32, 16, 128),
            pltpu.SemaphoreType.DMA((120,)),
        ],
        compiler_params=pltpu.CompilerParams(
            collective_id=0, has_side_effects=True, vmem_limit_bytes=54 * 1024 * 1024
        ),
        name="unet_step",
    )(noise_level, x, skip, cot, qkv_weight, out_weight, up_weight, conv_weight, film_scale, film_shift)
    outs = pl.pallas_call(
        unpack,
        out_shape=(
            cells, packed, cells, shape(768, 256), shape(256, 256), shape(128, 256), shape(9, 128, 128),
            shape(levels, 128), shape(levels, 128),
        ),
        in_specs=[ANY] * 5,
        out_specs=(ANY,) * 9,
        scratch_shapes=[
            bf(8, 128, 128), f32(8, 32, 256), bf(8, 128, 128), bf(2, 64, 16, 128), bf(96, 16, 128), f32(768, 256),
            f32(256, 256), f32(128, 256), f32(9, 128, 128), f32(levels, 128), f32(levels, 128),
            pltpu.SemaphoreType.DMA((14,)),
        ],
        compiler_params=pltpu.CompilerParams(vmem_limit_bytes=62 * 1024 * 1024),
        name="unpack",
    )(*parts)
    decoded, grad_x, grad_skip = outs[:3]
    return (
        jnp.transpose(decoded.reshape(8, 2, 64, 128), (0, 3, 1, 2)),
        jnp.transpose(grad_x.reshape(8, 1, 32, 256), (0, 3, 1, 2)),
        jnp.transpose(grad_skip.reshape(8, 2, 64, 128), (0, 3, 1, 2)),
    ) + tuple(outs[3:])


def solution(mesh):
    cells = P(None, None, "rows", "cols")
    return jax.shard_map(
        on_device,
        mesh=mesh,
        in_specs=(cells, cells, cells) + (P(),) * 7,
        out_specs=(cells, cells, cells) + (P(),) * 6,
        check_vma=False,
    )
```

```python
import functools

import jax
import jax.numpy as jnp
from jax import lax
from jax.experimental import pallas as pl
from jax.experimental.pallas import tpu as pltpu
from jax.sharding import PartitionSpec as P

MESH = pl.DeviceIdType.MESH
BF = jnp.bfloat16
F32 = jnp.float32
ROWS, COLS = 16, 8
HEADS = 4
BLOCK = 256
CHUNK = 1024
TAPS = [(-1, -1), (-1, 0), (-1, 1), (0, -1), (0, 0), (0, 1), (1, -1), (1, 0), (1, 1)]
VMEM = pl.BlockSpec(memory_space=pltpu.VMEM)
ANY = pl.BlockSpec(memory_space=pltpu.HBM)


def nn(a, b):
    return lax.dot_general(a, b, (((1,), (0,)), ((), ())), preferred_element_type=F32)


def nt(a, b):
    return lax.dot_general(a, b, (((1,), (1,)), ((), ())), preferred_element_type=F32)


def remote(src, dst, send, recv, row, col):
    return pltpu.make_async_remote_copy(
        src_ref=src, dst_ref=dst, send_sem=send, recv_sem=recv, device_id=(row, col), device_id_type=MESH
    )


def send_or_keep(here, src, dst, send, recv, row, col):
    @pl.when(here)
    def _():
        pltpu.make_async_copy(src, dst, recv).start()

    @pl.when(jnp.logical_not(here))
    def _():
        remote(src, dst, send, recv, row, col).start()


def drain(ref, sem):
    pltpu.make_async_copy(ref, ref, sem).wait()


def loop(lo, hi, body):
    def step(i, carry):
        body(i)
        return carry

    lax.fori_loop(lo, hi, step, 0)


def kernel(
    noise_hbm, x_hbm, skip_hbm, cot_hbm, wqkv_hbm, wout_hbm, wup_hbm, wconv_hbm, fscale_hbm, fshift_hbm,
    dec_hbm, gb_hbm, gskip_hbm, eag_hbm, lag_hbm,
    dec_ref, gb_ref, gskip_ref, eag, lag, noise, x_ref, skip_ref, cot_ref, wqkv, wout, wup, wconv, fscale, fshift,
    woutn, wq, wkv, kv_send, q_send, kv_in, q_fold, q_in, v1, xall, s_ref, top_ref, p_ref, invl_ref, o_buf, o_send, o_fold,
    ocell, gx, hx, gt, gedge, hedge, ghalo, hhalo, pre_ref, act_ref, dh_ref, dy_ref, du_ref,
    do_send, do_fold, ext_ref, qt_ref, dot_ref, dkvt, dq_acc, dq_send, dq_fold, dq_in, pair_send, pair_in, dkv_send,
    dkv_in, gacc, gkv, eg, epin, ehs, ersin, lg, lrs, sems,
):
    r, c = lax.axis_index("rows"), lax.axis_index("cols")
    par = lax.rem(r, 2)
    mate = r + 1 - 2 * par
    pair = lax.div(r, 2)
    kslot = pair * COLS + c
    head, quarter = lax.div(r, 4), lax.rem(r, 4)
    zhi, group = lax.rem(pair, 2), lax.div(pair, 4)
    qslot = lax.rem(pair, 4) * COLS + c
    own = zhi == group
    spot = c * HEADS + head
    sign = 1 - 2 * par
    cols = [lax.rem(c + COLS + sign * j, COLS) for j in range(COLS)]

    def pair_at(i):
        return lax.rem(pair + 8 + sign * i, 8)

    loads = [
        pltpu.make_async_copy(src, dst, sems.at[104 + i])
        for i, (src, dst) in enumerate((
            (x_hbm, x_ref), (wqkv_hbm, wqkv), (cot_hbm, cot_ref), (skip_hbm, skip_ref), (wout_hbm, wout),
            (wup_hbm, wup), (wconv_hbm, wconv), (fscale_hbm, fscale), (fshift_hbm, fshift), (noise_hbm, noise),
        ))
    ]
    for load in loads:
        load.start()

    barrier = pltpu.get_barrier_semaphore()

    def signal(row, dc):
        pl.semaphore_signal(barrier, inc=1, device_id=(row, dc), device_id_type=MESH)

    for j in range(1, COLS):
        signal(r, cols[j])

    def signal_row(i):
        row = lax.rem(r + i, ROWS)
        for j in range(COLS):
            signal(row, cols[j])

    loop(1, ROWS, signal_row)

    def to_attention(src, dst, send, recv):
        def row(i):
            h = lax.rem(head + i, HEADS)
            dr = HEADS * h + 2 * group + par
            send_or_keep((i == 0) & own, src.at[c * HEADS + h], dst.at[qslot], send, recv, dr, c)
            for j in range(1, COLS):
                remote(src.at[cols[j] * HEADS + h], dst.at[qslot], send, recv, dr, cols[j]).start()

        loop(0, HEADS, row)

    def to_cells(src, dst, send, recv, row):
        dr = 2 * (4 * zhi + row) + par
        send_or_keep(dr == r, src.at[row * COLS + c], dst.at[spot], send, recv, dr, c)
        for j in range(1, COLS):
            remote(src.at[row * COLS + cols[j]], dst.at[spot], send, recv, dr, cols[j]).start()

    def drain32(ref, sem):
        @pl.when(own)
        def _():
            drain(ref.at[pl.ds(0, 31)], sem)

        @pl.when(jnp.logical_not(own))
        def _():
            drain(ref, sem)

    def to_parity(lo, hi, source, target, send, recv, first=0, last=COLS):
        def row(i):
            at = pair_at(i)
            dr = 2 * at + par
            got = recv(i) if callable(recv) else recv
            for j in range(first, last):
                src = source(at, cols[j])
                if j == 0:
                    send_or_keep(i == 0, src, target, send, got, dr, c)
                else:
                    remote(src, target, send, got, dr, cols[j]).start()

        loop(lo, hi, row)

    def halo_start(ext, edge, halo, base):
        up, down = lax.rem(r + ROWS - 1, ROWS), lax.rem(r + 1, ROWS)
        left, right = lax.rem(c + COLS - 1, COLS), lax.rem(c + 1, COLS)
        copies = [
            remote(ext.at[:, 1, pl.ds(1, 2)], ext.at[:, 3, pl.ds(1, 2)], sems.at[base], sems.at[base + 1], up, c),
            remote(ext.at[:, 2, pl.ds(1, 2)], ext.at[:, 0, pl.ds(1, 2)], sems.at[base + 2], sems.at[base + 3], down, c),
        ]
        at = base + 4
        for row, slot in ((up, 2), (r, 1), (down, 0)):
            copies.append(remote(edge.at[0], halo.at[1, slot], sems.at[at], sems.at[at + 1], row, left))
            copies.append(remote(edge.at[1], halo.at[0, slot], sems.at[at + 2], sems.at[at + 3], row, right))
            at += 4
        for copy in copies:
            copy.start()
        return copies

    def halo_finish(ext, halo, copies):
        for copy in copies:
            copy.wait()

        @pl.when(r == 0)
        def _():
            ext[:, 0, 1:3] = jnp.zeros((8, 2, 32, 128), BF)
            halo[:, 0] = jnp.zeros((2, 2, 8, 128), F32)

        @pl.when(r == ROWS - 1)
        def _():
            ext[:, 3, 1:3] = jnp.zeros((8, 2, 32, 128), BF)
            halo[:, 2] = jnp.zeros((2, 2, 8, 128), F32)

        @pl.when(c == 0)
        def _():
            halo[0] = jnp.zeros((3, 2, 8, 128), F32)

        @pl.when(c == COLS - 1)
        def _():
            halo[1] = jnp.zeros((3, 2, 8, 128), F32)

        place = lax.broadcasted_iota(jnp.int32, (32, 128), 0)

        def one(s):
            for row, (slot, a) in enumerate(((0, 1), (1, 0), (1, 1), (2, 0))):
                odd = ext[s, row, 2].astype(F32)
                even = ext[s, row, 1].astype(F32)
                before = halo[0, slot, a, pl.ds(s, 1), :]
                after = halo[1, slot, a, pl.ds(s, 1), :]
                ext[s, row, 0] = jnp.where(place == 0, before, pltpu.roll(odd, 1, axis=0)).astype(BF)
                ext[s, row, 3] = jnp.where(place == 31, after, pltpu.roll(even, 31, axis=0)).astype(BF)

        loop(0, 8, one)

    esem = [sems.at[48 + i] for i in range(8)]

    def early_put(at, value):
        n = value.shape[0] // 16
        eg[at // 64, at % 64 : at % 64 + n] = value.astype(BF).reshape(n, 16, 128)

    def early_halves():
        return remote(eg.at[1 - par], epin, esem[0], esem[1], mate, c)

    def early_scatter():
        early_halves().wait()
        ehs[...] = (eg[par].astype(F32) + epin[...].astype(F32)).astype(BF)
        to_parity(0, 8, lambda at, dc: ehs.at[at * COLS + dc], ersin.at[kslot], esem[2], esem[3])

    def early_gather():
        drain(ersin, esem[3])
        eag[par, kslot] = jnp.sum(ersin[...].astype(F32), axis=0).astype(BF)
        mine = eag.at[par, kslot]
        for j in range(1, COLS):
            remote(mine, mine, esem[4], esem[5], r, cols[j]).start()
        def row(i):
            dr = 2 * pair_at(i) + par
            for j in range(COLS):
                remote(mine, mine, esem[4], esem[5], dr, cols[j]).start()

        loop(1, 8, row)

    def early_swap():
        return remote(eag.at[par], eag.at[par], esem[6], esem[7], mate, c)

    def early_drain():
        drain(eag.at[0, pl.ds(0, 63)], esem[5])
        drain(ersin.at[pl.ds(0, 63)], esem[4])
        drain(ehs.at[pl.ds(0, 63)], esem[2])

    low_lane = lax.broadcasted_iota(jnp.int32, (BLOCK, 128), 1) < 64

    def half_turn(value):
        return pltpu.roll(value, 64, axis=1)

    def fold_low(value):
        cut = value.reshape(8, 32, 128)
        first, second = cut[:, 0:16].reshape(128, 128), cut[:, 16:32].reshape(128, 128)
        return jnp.where(low_lane[0:128], first, half_turn(second)).reshape(8, 16, 128)

    def fold_high(value):
        cut = value.reshape(8, 32, 128)
        first, second = cut[:, 0:16].reshape(128, 128), cut[:, 16:32].reshape(128, 128)
        return jnp.where(low_lane[0:128], half_turn(first), second).reshape(8, 16, 128)

    def unfold(src, dst, high, clear):
        def some(i):
            at = pl.ds(8 * i, 8)
            flat = src[at].reshape(128, 128).astype(F32)
            turned = half_turn(flat)
            first, second = (turned, flat) if high else (flat, turned)
            if clear:
                keep = jnp.logical_not(low_lane[0:128]) if high else low_lane[0:128]
                first, second = jnp.where(keep, first, 0.0), jnp.where(keep, second, 0.0)
            dst[at, 0:16] = first.astype(BF).reshape(8, 16, 128)
            dst[at, 16:32] = second.astype(BF).reshape(8, 16, 128)

        loop(0, 4, some)

    loads[0].wait()
    loads[1].wait()
    zero64 = jnp.zeros((64, 256), BF)
    for h in range(HEADS):
        wq[128 * h : 128 * h + 64] = (wqkv[64 * h : 64 * h + 64].astype(F32) * 0.125).astype(BF)
        wq[128 * h + 64 : 128 * h + 128] = zero64
        wkv[128 * h : 128 * h + 64] = wqkv[256 + 64 * h : 320 + 64 * h]
        wkv[128 * h + 64 : 128 * h + 128] = wqkv[512 + 64 * h : 576 + 64 * h]
    xt = x_ref[...].reshape(256, 256)
    for h in range(HEADS):
        rows = slice(128 * h, 128 * h + 128)
        kv = nt(xt, wkv[rows, :]).astype(BF).reshape(8, 32, 128)
        q = fold_low(nt(xt, wq[rows, :])).astype(BF)
        for s in range(8):
            kv_send[s * HEADS + h] = kv[s]
            q_send[s * HEADS + h] = q[s]

    to = lax.broadcasted_iota(jnp.int32, (128, 128), 0)
    of = lax.broadcasted_iota(jnp.int32, (128, 128), 1)
    split = (of == (lax.div(to, 64) * 64 + 2 * lax.rem(to, 32) + lax.rem(lax.div(to, 32), 2))).astype(BF)
    merge = (to == (lax.div(of, 64) * 64 + 2 * lax.rem(of, 32) + lax.rem(lax.div(of, 32), 2))).astype(BF)
    eye = (to == of).astype(BF)

    def take_cot(s):
        g = nn(split, cot_ref[s])
        low = g.astype(BF)
        gx[s, 1:3, 1:3] = low.reshape(2, 2, 32, 128)
        gt[s] = nt(eye, low).astype(BF)
        for a in range(2):
            gedge[0, a, pl.ds(s, 1), :] = g[64 * a : 64 * a + 1]
            gedge[1, a, pl.ds(s, 1), :] = g[64 * a + 63 : 64 * a + 64]

    pl.semaphore_wait(barrier, ROWS * COLS - 1)
    to_attention(q_send, q_fold, sems.at[2], sems.at[3])
    to_parity(
        0, 8, lambda at, dc: kv_send.at[dc * HEADS + lax.div(at, 2)], kv_in.at[par, kslot], sems.at[0],
        lambda i: sems.at[80 + i],
    )
    loads[2].wait()
    loop(0, 8, take_cot)
    cot_copies = halo_start(gx, gedge, ghalo, 16)
    for load in loads[3:]:
        load.wait()

    def take_skip(s):
        pre_ref[s] = nn(split, skip_ref[s])

    loop(0, 8, take_skip)
    for g in range(2):
        block = wout[:, 128 * g : 128 * (g + 1)].astype(F32)
        woutn[:, 256 * g : 256 * g + 128] = jnp.where(low_lane, 0.0, half_turn(block)).astype(BF)
        woutn[:, 256 * g + 128 : 256 * g + 256] = jnp.where(low_lane, 0.0, block).astype(BF)

    def back_conv(half):
        total = jnp.zeros((512, 128), F32)
        for t, (dr, dc) in enumerate(TAPS):
            window = gx[pl.ds(4 * half, 4), 1 - dr : 3 - dr, 1 - dc : 3 - dc].reshape(512, 128)
            total = total + nn(window, wconv[t])
        dh_ref[pl.ds(4 * half, 4)] = total.reshape(4, 128, 128)

    drain(q_fold, sems.at[3])
    unfold(q_fold, q_in, False, True)
    top_ref[...] = jnp.full((1024, 128), -jnp.inf, F32)

    def score(half, at):
        part = kv_in[half, pl.ds(COLS * at, COLS)].reshape(256, 128)
        place = pl.multiple_of(half * 2048 + at * 256, 256)
        v1[pl.ds(place, 256), :] = jnp.where(low_lane, jnp.ones_like(part), part)
        for b in range(4):
            rows = slice(BLOCK * b, BLOCK * (b + 1))
            s = nt(q_in[8 * b : 8 * b + 8].reshape(BLOCK, 128), part)
            s_ref[rows, pl.ds(place, 256)] = s
            top_ref[rows, :] = jnp.maximum(top_ref[rows, :], jnp.maximum(s[:, 0:128], s[:, 128:256]))

    def mate_group(i):
        at = kv_in.at[par, pl.ds(COLS * lax.rem(pair + 8 - sign * i, 8), COLS)]
        return remote(at, at, sems.at[88 + i], sems.at[96 + i], mate, c)

    def take_group(i):
        at = lax.rem(pair + 8 - sign * i, 8)
        drain(kv_in.at[par, pl.ds(COLS * at, COLS)], sems.at[80 + i])
        mate_group(i).start()
        score(par, at)

    def take_mate(i):
        mate_group(i).wait()
        score(1 - par, pair_at(i))

    take_group(0)

    def both(i):
        take_group(i)
        take_mate(i - 1)

    loop(1, 8, both)
    to_parity(0, 8, lambda at, dc: x_ref.at[dc], xall.at[kslot], sems.at[60], sems.at[61], 0, 4)
    take_mate(7)
    for _ in range(3):
        drain(kv_send.at[pl.ds(0, 21)], sems.at[0])
    drain32(q_send, sems.at[2])

    def forward(b):
        rows = pl.ds(pl.multiple_of(b * BLOCK, BLOCK), BLOCK)
        m = jnp.max(top_ref[rows, :], axis=1, keepdims=True)
        acc = jnp.zeros((BLOCK, 128), F32)
        for j in range(4096 // CHUNK):
            p = jnp.exp(s_ref[rows, CHUNK * j : CHUNK * (j + 1)] - m).astype(BF)
            p_ref[rows, CHUNK * j : CHUNK * (j + 1)] = p
            acc = acc + nn(p, v1[CHUNK * j : CHUNK * (j + 1), :])
        inv = 1.0 / jnp.where(low_lane, 1.0, half_turn(acc))
        invl_ref[rows, :] = inv
        o = jnp.where(low_lane, 0.0, acc * inv)
        o_buf[rows, :] = o.astype(BF)
        o_send[pl.ds(8 * b, 8)] = fold_high(o).astype(BF)
        to_cells(o_send, o_fold, sems.at[6], sems.at[7], b)

    loop(0, 1024 // BLOCK, forward)
    halo_finish(gx, ghalo, cot_copies)
    loop(0, 2, back_conv)

    levels = fscale.shape[0]
    level = lax.broadcasted_iota(jnp.int32, (levels, 128), 0)
    scales, shifts = [], []
    for s in range(8):
        here = level == noise[s]
        scales.append(1.0 + jnp.sum(jnp.where(here, fscale[...], 0.0), axis=0, keepdims=True))
        shifts.append(jnp.sum(jnp.where(here, fshift[...], 0.0), axis=0, keepdims=True))
    drain(o_fold, sems.at[7])
    drain32(o_send, sems.at[6])
    unfold(o_fold, ocell, True, False)
    oc = ocell[...].reshape(8, HEADS, 32, 128)
    branch = x_ref[...].reshape(256, 256).astype(F32)
    for h in range(HEADS):
        branch = branch + nt(oc[:, h].reshape(256, 128), woutn[:, 128 * h : 128 * (h + 1)])
    y = branch.astype(BF)
    lifted = nt(y, wup[...])
    for s in range(8):
        u = lifted[32 * s : 32 * (s + 1)]
        pre = pre_ref[s] + jnp.concatenate([u, u, u, u], axis=0)
        pre_ref[s] = pre
        act = pre * scales[s] + shifts[s]
        act_ref[s] = act
        low = (act * jax.nn.sigmoid(act)).astype(BF)
        hx[s, 1:3, 1:3] = low.reshape(2, 2, 32, 128)
        wide = low.astype(F32)
        for a in range(2):
            hedge[0, a, s : s + 1, :] = wide[64 * a : 64 * a + 1]
            hedge[1, a, s : s + 1, :] = wide[64 * a + 63 : 64 * a + 64]
    hid_copies = halo_start(hx, hedge, hhalo, 32)

    spread = lax.broadcasted_iota(jnp.int32, (32, 128), 0)
    scale_sum, shift_sum = jnp.zeros((32, 128), F32), jnp.zeros((32, 128), F32)
    for s in range(8):
        act = act_ref[s]
        sg = jax.nn.sigmoid(act)
        dact = dh_ref[s] * (sg * (1.0 + act * (1.0 - sg)))
        here = spread == noise[s]
        scale_sum += jnp.where(here, jnp.sum(dact * pre_ref[s], axis=0, keepdims=True), 0.0)
        shift_sum += jnp.where(here, jnp.sum(dact, axis=0, keepdims=True), 0.0)
        dpre = dact * scales[s]
        dh_ref[s] = dpre
        du_ref[32 * s : 32 * (s + 1)] = dpre[0:32] + dpre[32:64] + dpre[64:96] + dpre[96:128]
    du = du_ref[...].astype(BF)
    dy = nn(du, wup[...])
    dy_ref[...] = dy
    low_dy = dy.astype(BF)
    for h in range(HEADS):
        do = fold_high(nn(low_dy, woutn[:, 128 * h : 128 * (h + 1)])).astype(BF)
        for s in range(8):
            do_send[s * HEADS + h] = do[s]
    to_attention(do_send, do_fold, sems.at[8], sems.at[9])
    to_parity(0, 8, lambda at, dc: x_ref.at[dc], xall.at[kslot], sems.at[60], sems.at[61], 4, 8)

    early_put(120, scale_sum)
    early_put(122, shift_sum)
    grad_up = nn(du_ref[...].T.astype(BF), y)
    early_put(72, grad_up[:, 0:128])
    early_put(80, grad_up[:, 128:256])
    dyt = dy.T.astype(BF)
    for g in range(2):
        first = nn(dyt, oc[:, 2 * g].reshape(256, 128))
        second = nn(dyt, oc[:, 2 * g + 1].reshape(256, 128))
        early_put(88 + 16 * g, jnp.where(low_lane, half_turn(first), second))

    halo_finish(hx, hhalo, hid_copies)

    def weight_grad(half):
        grads = [gt[4 * half + i] for i in range(4)]
        for t, (dr, dc) in enumerate(TAPS):
            window = hx[pl.ds(4 * half, 4), 1 + dr : 3 + dr, 1 + dc : 3 + dc]
            term = None
            for i in range(4):
                one = nn(grads[i], window[i].reshape(128, 128))
                term = one if term is None else term + one
            gacc[t] = gacc[t] + term

    def conv(half):
        total = jnp.zeros((512, 128), F32)
        for t, (dr, dc) in enumerate(TAPS):
            window = hx[pl.ds(4 * half, 4), 1 + dr : 3 + dr, 1 + dc : 3 + dc]
            total = total + nt(window.reshape(512, 128), wconv[t])
        low = total.astype(BF)
        for i in range(4):
            dec_ref[4 * half + i] = nn(merge, low[128 * i : 128 * (i + 1)]).astype(BF)
            gskip_ref[4 * half + i] = nn(merge, dh_ref[4 * half + i].astype(BF)).astype(BF)

    gacc[...] = jnp.zeros((9, 128, 128), F32)
    loop(0, 2, weight_grad)

    def turn_queries(b):
        q = q_in[pl.ds(8 * b, 8)].reshape(BLOCK, 128)
        qt_ref[b] = q.astype(F32).T[0:64].astype(BF)

    loop(0, 4, turn_queries)
    for t in range(9):
        early_put(8 * t, gacc[t])
    for k in range(124, 128):
        eg[1, k - 64] = jnp.zeros((16, 128), BF)
    early_halves().start()

    drain(do_fold, sems.at[9])
    drain32(do_send, sems.at[8])
    unfold(do_fold, ocell, True, True)
    lane = lax.broadcasted_iota(jnp.int32, (BLOCK, 128), 1)

    def prepare(b):
        rows = pl.ds(pl.multiple_of(b * BLOCK, BLOCK), BLOCK)
        do = (ocell[pl.ds(8 * b, 8)].reshape(BLOCK, 128).astype(F32) * invl_ref[rows, :]).astype(BF)
        dof = do.astype(F32)
        delta = -jnp.sum(dof * o_buf[rows, :].astype(F32), axis=1, keepdims=True)
        high = delta.astype(BF).astype(F32)
        mid = (delta - high).astype(BF).astype(F32)
        rest = delta - high - mid
        ext = jnp.where(lane == 0, high, jnp.where(lane == 1, mid, jnp.where(lane == 2, rest, dof)))
        ext_ref[rows, :] = ext.astype(BF)
        dot_ref[b] = dof.T[64:128].astype(BF)
        dq_acc[rows, :] = jnp.zeros((BLOCK, 128), F32)

    loop(0, 4, prepare)
    gkv[...] = jnp.zeros((256, 256), F32)
    early_scatter()

    def backward(half, j):
        at = pl.multiple_of(half * 2048 + j * CHUNK, CHUNK)
        kc = kv_in[half, pl.ds(32 * j, 32)].reshape(CHUNK, 128)
        vc = v1[pl.ds(at, CHUNK), :]
        for b in range(4):
            rows = slice(BLOCK * b, BLOCK * (b + 1))
            p = p_ref[rows, pl.ds(at, CHUNK)]
            ds = (p.astype(F32) * nt(ext_ref[rows, :], vc)).astype(BF)
            dq_acc[rows, :] += nn(ds, kc)
            for lo, lhs, rhs in ((0, qt_ref, ds), (64, dot_ref, p)):
                part = nn(lhs[b], rhs)
                dkvt[lo : lo + 64] = part if b == 0 else dkvt[lo : lo + 64] + part

    def pair_copy(j):
        return remote(pair_send.at[j], pair_in.at[j], sems.at[10 + j], sems.at[12 + j], mate, c)

    def mate_chunk(j):
        backward(1 - par, j)
        pair_send[j] = dkvt[...].astype(BF)
        pair_copy(j).start()

    loop(0, 2, mate_chunk)

    def own_chunk(j):
        backward(par, j)
        pair_copy(j).wait()
        total = dkvt[...] + pair_in[j].astype(F32)
        dkv_send[pl.ds(32 * j, 32)] = total.T.astype(BF).reshape(32, 32, 128)
        target = dkv_in.at[zhi, spot]

        def row(i):
            rp = 4 * j + lax.rem(pair + i, 4)
            dr = 2 * rp + par
            send_or_keep(rp == pair, dkv_send.at[rp * COLS + c], target, sems.at[14], sems.at[15], dr, c)
            for k in range(1, COLS):
                remote(dkv_send.at[rp * COLS + cols[k]], target, sems.at[14], sems.at[15], dr, cols[k]).start()

        loop(0, 4, row)
        pair_send[j] = total.astype(BF)

    loop(0, 2, own_chunk)

    drain(xall, sems.at[61])
    drain(xall.at[pl.ds(0, 63)], sems.at[60])
    gkv[0:128] = nn(pair_send[0], xall[0:32].reshape(CHUNK, 256)) + nn(pair_send[1], xall[32:64].reshape(CHUNK, 256))
    for b in range(4):
        xq = xall[pl.ds(COLS * (4 * zhi + b), COLS)].reshape(BLOCK, 256)
        gkv[128:256] += nn(dq_acc[BLOCK * b : BLOCK * (b + 1), :].T.astype(BF), xq)

    for g in range(2):
        lanes = slice(128 * g, 128 * (g + 1))
        for part, (lo, factor) in enumerate(((128, 0.125), (0, 1.0), (64, 1.0))):
            piece = (gkv[lo : lo + 64, lanes] * factor).astype(BF)
            lg[12 * g + 4 * part : 12 * g + 4 * part + 4] = piece.reshape(4, 16, 128)

    member = quarter * COLS + c
    kind = head * COLS + c

    def send_lg(i):
        dr = HEADS * head + i
        send_or_keep(quarter == i, lg.at[i * COLS + c], lrs.at[member], sems.at[58], sems.at[59], dr, c)
        for j in range(1, COLS):
            remote(lg.at[i * COLS + cols[j]], lrs.at[member], sems.at[58], sems.at[59], dr, cols[j]).start()

    loop(0, 3, send_lg)

    def give_dq(b):
        rows = pl.ds(pl.multiple_of(b * BLOCK, BLOCK), BLOCK)
        dq_send[pl.ds(8 * b, 8)] = fold_low(dq_acc[rows, :]).astype(BF)
        to_cells(dq_send, dq_fold, sems.at[56], sems.at[57], b)

    loop(0, 4, give_dq)
    early_gather()
    loop(0, 2, conv)
    stores = [
        pltpu.make_async_copy(src, dst, sems.at[68 + i])
        for i, (src, dst) in enumerate((
            (dec_ref, dec_hbm), (gskip_ref, gskip_hbm), (gb_ref, gb_hbm), (eag, eag_hbm), (lag, lag_hbm),
        ))
    ]
    stores[0].start()
    stores[1].start()

    @pl.when(quarter < 3)
    def _():
        drain(lrs, sems.at[59])
        mine = lag.at[quarter * 32 + kind]
        lag[quarter * 32 + kind] = jnp.sum(lrs[...].astype(F32), axis=0).astype(BF)
        for j in range(1, COLS):
            remote(mine, mine, sems.at[64], sems.at[65], r, cols[j]).start()

        def row(i):
            dr = 2 * pair_at(i) + par
            for j in range(COLS):
                remote(mine, mine, sems.at[64], sems.at[65], dr, cols[j]).start()

        loop(1, 8, row)

    early_drain()
    last_swap = early_swap()
    last_swap.start()
    drain(dq_fold, sems.at[57])
    drain32(dq_send, sems.at[56])
    unfold(dq_fold, dq_in, False, False)
    drain(dkv_in, sems.at[15])
    drain(dkv_send.at[pl.ds(0, 63)], sems.at[14])
    dq_all = dq_in[...].reshape(8, HEADS, 32, 128)
    dkv_all = (dkv_in[0].astype(F32) + dkv_in[1].astype(F32)).astype(BF).reshape(8, HEADS, 32, 128)
    grad = dy_ref[...]
    for h in range(HEADS):
        rows = slice(128 * h, 128 * h + 128)
        grad = grad + nn(dq_all[:, h].reshape(256, 128), wq[rows, :])
        grad = grad + nn(dkv_all[:, h].reshape(256, 128), wkv[rows, :])
    gb_ref[...] = grad.reshape(8, 32, 256)
    stores[2].start()
    last_swap.wait()
    stores[3].start()

    @pl.when(quarter < 3)
    def _():
        drain(lg.at[pl.ds(0, 23)], sems.at[58])
        drain(lrs, sems.at[64])
        drain(lrs.at[pl.ds(0, 31)], sems.at[64])

    @pl.when(quarter == 3)
    def _():
        drain(lg, sems.at[58])
        drain(lag.at[pl.ds(0, 32)], sems.at[65])

    @pl.when(quarter == 1)
    def _():
        drain(lag.at[pl.ds(0, 31)], sems.at[65])

    def forward_sums(at):
        part = lag.at[pl.ds(at, 32)]
        remote(part, part, sems.at[66], sems.at[67], mate, c).start()

    @pl.when(par == 0)
    def _():
        drain(lag.at[pl.ds(0, 63)], sems.at[65])
        forward_sums(0)
        forward_sums(64)
        drain(lag.at[pl.ds(0, 64)], sems.at[66])
        drain(lag.at[pl.ds(0, 32)], sems.at[67])

    @pl.when(par == 1)
    def _():
        forward_sums(32)
        drain(lag.at[pl.ds(0, 32)], sems.at[66])
        drain(lag.at[pl.ds(0, 64)], sems.at[67])

    stores[4].start()
    for store in stores:
        store.wait()


def unpack(
    dec, gb, gskip, eag, lag, dec_ref, gb_ref, gskip_ref, gqkv_ref, gout_ref, gup_ref, gconv_ref, gscale_ref, gshift_ref,
    dec_v, gb_v, gskip_v, eag_v, lag_v, gqkv_v, gout_v, gup_v, gconv_v, gscale_v, gshift_v, sems,
):
    held = (dec_v, gb_v, gskip_v, eag_v, lag_v)
    loads = [
        pltpu.make_async_copy(src, dst, sems.at[i]) for i, (src, dst) in enumerate(zip((dec, gb, gskip, eag, lag), held))
    ]
    for load in loads:
        load.start()
    stores = [
        pltpu.make_async_copy(src, dst, sems.at[5 + i])
        for i, (src, dst) in enumerate((
            (dec_v, dec_ref), (gb_v, gb_ref), (gskip_v, gskip_ref), (gconv_v, gconv_ref), (gscale_v, gscale_ref),
            (gshift_v, gshift_ref), (gup_v, gup_ref), (gout_v, gout_ref), (gqkv_v, gqkv_ref),
        ))
    ]
    loads[3].wait()

    def early(at, n):
        return eag_v[at // 64, at % 64 : at % 64 + n].reshape(n * 16, 128).astype(F32)

    for t in range(9):
        gconv_v[t] = early(8 * t, 8)
    stores[3].start()
    levels = gscale_v.shape[0]
    gscale_v[...] = early(120, 2)[0:levels]
    gshift_v[...] = early(122, 2)[0:levels]
    for g in range(2):
        lanes = slice(128 * g, 128 * (g + 1))
        gup_v[:, lanes] = early(72 + 8 * g, 8)
        gout_v[:, lanes] = early(88 + 16 * g, 16)
    for i in range(4, 8):
        stores[i].start()
    loads[4].wait()
    for g in range(2):
        lanes = slice(128 * g, 128 * (g + 1))
        for part in range(3):
            for h in range(HEADS):
                piece = 12 * g + 4 * part
                at = 32 * (piece // 8) + 8 * h + piece % 8
                rows = slice(256 * part + 64 * h, 256 * part + 64 * h + 64)
                gqkv_v[rows, lanes] = lag_v[at : at + 4].reshape(64, 128).astype(F32)
    stores[8].start()
    for i in range(3):
        loads[i].wait()
        stores[i].start()
    for store in stores:
        store.wait()


def on_device(
    bottleneck, skip_field, cotangent, noise_level, qkv_weight, out_weight, up_weight, conv_weight,
    film_scale, film_shift,
):
    levels = film_scale.shape[0]
    x = jnp.transpose(bottleneck, (0, 2, 3, 1)).reshape(8, 32, 256)
    skip = jnp.transpose(skip_field, (0, 2, 3, 1)).reshape(8, 128, 128)
    cot = jnp.transpose(cotangent, (0, 2, 3, 1)).reshape(8, 128, 128)

    def shape(*dims, kind=F32):
        return jax.ShapeDtypeStruct(dims, kind)

    def bf(*dims):
        return pltpu.VMEM(dims, BF)

    def f32(*dims):
        return pltpu.VMEM(dims, F32)

    packet, folded = (32, 32, 128), (32, 16, 128)
    cells, packed = shape(8, 128, 128, kind=BF), shape(8, 32, 256)
    parts = pl.pallas_call(
        kernel,
        out_shape=(cells, packed, cells, shape(2, 64, 16, 128, kind=BF), shape(96, 16, 128, kind=BF)),
        in_specs=[ANY] * 10,
        out_specs=(ANY,) * 5,
        scratch_shapes=[
            bf(8, 128, 128), f32(8, 32, 256), bf(8, 128, 128), bf(2, 64, 16, 128), bf(96, 16, 128),
            pltpu.SMEM((8,), jnp.int32), bf(8, 32, 256), bf(8, 128, 128), bf(8, 128, 128), bf(768, 256), bf(256, 256),
            bf(128, 256), bf(9, 128, 128), f32(levels, 128), f32(levels, 128),
            bf(256, 512), bf(512, 256), bf(512, 256), bf(*packet), bf(*folded), bf(2, 64, 32, 128), bf(*folded),
            bf(*packet), bf(4096, 128), bf(64, 32, 256), f32(1024, 4096), f32(1024, 128), bf(1024, 4096), f32(1024, 128),
            bf(1024, 128), bf(*folded), bf(*folded),
            bf(*packet), bf(8, 4, 4, 32, 128), bf(8, 4, 4, 32, 128), bf(8, 128, 128),
            f32(2, 2, 8, 128), f32(2, 2, 8, 128), f32(2, 3, 2, 8, 128), f32(2, 3, 2, 8, 128),
            f32(8, 128, 128), f32(8, 128, 128), f32(8, 128, 128), f32(256, 256), f32(256, 128),
            bf(*folded), bf(*folded), bf(1024, 128), bf(4, 64, 256), bf(4, 64, 256), f32(128, CHUNK),
            f32(1024, 128), bf(*folded), bf(*folded), bf(*packet),
            bf(2, 128, CHUNK), bf(2, 128, CHUNK), bf(64, 32, 128), bf(2, 32, 32, 128), f32(9, 128, 128), f32(256, 256),
            bf(2, 64, 16, 128), bf(64, 16, 128), bf(64, 16, 128), bf(64, 16, 128),
            bf(24, 16, 128), bf(32, 16, 128),
            pltpu.SemaphoreType.DMA((120,)),
        ],
        compiler_params=pltpu.CompilerParams(
            collective_id=0, has_side_effects=True, vmem_limit_bytes=54 * 1024 * 1024
        ),
        name="unet_step",
    )(noise_level, x, skip, cot, qkv_weight, out_weight, up_weight, conv_weight, film_scale, film_shift)
    outs = pl.pallas_call(
        unpack,
        out_shape=(
            cells, packed, cells, shape(768, 256), shape(256, 256), shape(128, 256), shape(9, 128, 128),
            shape(levels, 128), shape(levels, 128),
        ),
        in_specs=[ANY] * 5,
        out_specs=(ANY,) * 9,
        scratch_shapes=[
            bf(8, 128, 128), f32(8, 32, 256), bf(8, 128, 128), bf(2, 64, 16, 128), bf(96, 16, 128), f32(768, 256),
            f32(256, 256), f32(128, 256), f32(9, 128, 128), f32(levels, 128), f32(levels, 128),
            pltpu.SemaphoreType.DMA((14,)),
        ],
        compiler_params=pltpu.CompilerParams(vmem_limit_bytes=62 * 1024 * 1024),
        name="unpack",
    )(*parts)
    decoded, grad_x, grad_skip = outs[:3]
    return (
        jnp.transpose(decoded.reshape(8, 2, 64, 128), (0, 3, 1, 2)),
        jnp.transpose(grad_x.reshape(8, 1, 32, 256), (0, 3, 1, 2)),
        jnp.transpose(grad_skip.reshape(8, 2, 64, 128), (0, 3, 1, 2)),
    ) + tuple(outs[3:])


def solution(mesh):
    cells = P(None, None, "rows", "cols")
    return jax.shard_map(
        on_device,
        mesh=mesh,
        in_specs=(cells, cells, cells) + (P(),) * 7,
        out_specs=(cells, cells, cells) + (P(),) * 6,
        check_vma=False,
    )
```

```python
import functools

import jax
import jax.numpy as jnp
from jax import lax
from jax.experimental import pallas as pl
from jax.experimental.pallas import tpu as pltpu
from jax.sharding import PartitionSpec as P

MESH = pl.DeviceIdType.MESH
BF = jnp.bfloat16
F32 = jnp.float32
ROWS, COLS = 16, 8
HEADS = 4
BLOCK = 256
CHUNK = 1024
TAPS = [(-1, -1), (-1, 0), (-1, 1), (0, -1), (0, 0), (0, 1), (1, -1), (1, 0), (1, 1)]
VMEM = pl.BlockSpec(memory_space=pltpu.VMEM)
ANY = pl.BlockSpec(memory_space=pltpu.HBM)


def nn(a, b):
    return lax.dot_general(a, b, (((1,), (0,)), ((), ())), preferred_element_type=F32)


def nt(a, b):
    return lax.dot_general(a, b, (((1,), (1,)), ((), ())), preferred_element_type=F32)


def remote(src, dst, send, recv, row, col):
    return pltpu.make_async_remote_copy(
        src_ref=src, dst_ref=dst, send_sem=send, recv_sem=recv, device_id=(row, col), device_id_type=MESH
    )


def send_or_keep(here, src, dst, send, recv, row, col):
    @pl.when(here)
    def _():
        pltpu.make_async_copy(src, dst, recv).start()

    @pl.when(jnp.logical_not(here))
    def _():
        remote(src, dst, send, recv, row, col).start()


def drain(ref, sem):
    pltpu.make_async_copy(ref, ref, sem).wait()


def loop(lo, hi, body):
    def step(i, carry):
        body(i)
        return carry

    lax.fori_loop(lo, hi, step, 0)


def kernel(
    noise_hbm, x_hbm, skip_hbm, cot_hbm, wqkv_hbm, wout_hbm, wup_hbm, wconv_hbm, fscale_hbm, fshift_hbm,
    dec_hbm, gb_hbm, gskip_hbm, eag_hbm, lag_hbm,
    dec_ref, gb_ref, gskip_ref, eag, lag, noise, x_ref, skip_ref, cot_ref, wqkv, wout, wup, wconv, fscale, fshift,
    woutn, wq, wkv, kv_send, q_send, kv_in, q_fold, q_in, v1, xall, s_ref, top_ref, p_ref, invl_ref, o_buf, o_send, o_fold,
    ocell, gx, hx, gt, gedge, hedge, ghalo, hhalo, pre_ref, act_ref, dh_ref, dy_ref, du_ref,
    do_send, do_fold, ext_ref, qt_ref, dot_ref, dkvt, dq_acc, dq_send, dq_fold, dq_in, pair_send, pair_in, dkv_send,
    dkv_in, gacc, gkv, eg, epin, ehs, ersin, lg, lrs, sems,
):
    r, c = lax.axis_index("rows"), lax.axis_index("cols")
    par = lax.rem(r, 2)
    mate = r + 1 - 2 * par
    pair = lax.div(r, 2)
    kslot = pair * COLS + c
    head, quarter = lax.div(r, 4), lax.rem(r, 4)
    zhi, group = lax.rem(pair, 2), lax.div(pair, 4)
    qslot = lax.rem(pair, 4) * COLS + c
    own = zhi == group
    spot = c * HEADS + head
    sign = 1 - 2 * par
    cols = [lax.rem(c + COLS + sign * j, COLS) for j in range(COLS)]

    def pair_at(i):
        return lax.rem(pair + 8 + sign * i, 8)

    loads = [
        pltpu.make_async_copy(src, dst, sems.at[104 + i])
        for i, (src, dst) in enumerate((
            (x_hbm, x_ref), (wqkv_hbm, wqkv), (cot_hbm, cot_ref), (skip_hbm, skip_ref), (wout_hbm, wout),
            (wup_hbm, wup), (wconv_hbm, wconv), (fscale_hbm, fscale), (fshift_hbm, fshift), (noise_hbm, noise),
        ))
    ]
    for load in loads:
        load.start()

    barrier = pltpu.get_barrier_semaphore()

    def signal(row, dc):
        pl.semaphore_signal(barrier, inc=1, device_id=(row, dc), device_id_type=MESH)

    for j in range(1, COLS):
        signal(r, cols[j])

    def signal_row(i):
        row = lax.rem(r + i, ROWS)
        for j in range(COLS):
            signal(row, cols[j])

    loop(1, ROWS, signal_row)

    def to_attention(src, dst, send, recv):
        def row(i):
            h = lax.rem(head + i, HEADS)
            dr = HEADS * h + 2 * group + par
            send_or_keep((i == 0) & own, src.at[c * HEADS + h], dst.at[qslot], send, recv, dr, c)
            for j in range(1, COLS):
                remote(src.at[cols[j] * HEADS + h], dst.at[qslot], send, recv, dr, cols[j]).start()

        loop(0, HEADS, row)

    def to_cells(src, dst, send, recv, row):
        dr = 2 * (4 * zhi + row) + par
        send_or_keep(dr == r, src.at[row * COLS + c], dst.at[spot], send, recv, dr, c)
        for j in range(1, COLS):
            remote(src.at[row * COLS + cols[j]], dst.at[spot], send, recv, dr, cols[j]).start()

    def drain32(ref, sem):
        @pl.when(own)
        def _():
            drain(ref.at[pl.ds(0, 31)], sem)

        @pl.when(jnp.logical_not(own))
        def _():
            drain(ref, sem)

    def to_parity(lo, hi, source, target, send, recv, first=0, last=COLS):
        def row(i):
            at = pair_at(i)
            dr = 2 * at + par
            got = recv(i) if callable(recv) else recv
            for j in range(first, last):
                src = source(at, cols[j])
                if j == 0:
                    send_or_keep(i == 0, src, target, send, got, dr, c)
                else:
                    remote(src, target, send, got, dr, cols[j]).start()

        loop(lo, hi, row)

    def halo_start(ext, edge, halo, base):
        up, down = lax.rem(r + ROWS - 1, ROWS), lax.rem(r + 1, ROWS)
        left, right = lax.rem(c + COLS - 1, COLS), lax.rem(c + 1, COLS)
        copies = [
            remote(ext.at[:, 1, pl.ds(1, 2)], ext.at[:, 3, pl.ds(1, 2)], sems.at[base], sems.at[base + 1], up, c),
            remote(ext.at[:, 2, pl.ds(1, 2)], ext.at[:, 0, pl.ds(1, 2)], sems.at[base + 2], sems.at[base + 3], down, c),
        ]
        at = base + 4
        for row, slot in ((up, 2), (r, 1), (down, 0)):
            copies.append(remote(edge.at[0], halo.at[1, slot], sems.at[at], sems.at[at + 1], row, left))
            copies.append(remote(edge.at[1], halo.at[0, slot], sems.at[at + 2], sems.at[at + 3], row, right))
            at += 4
        for copy in copies:
            copy.start()
        return copies

    def halo_finish(ext, halo, copies):
        for copy in copies:
            copy.wait()

        @pl.when(r == 0)
        def _():
            ext[:, 0, 1:3] = jnp.zeros((8, 2, 32, 128), BF)
            halo[:, 0] = jnp.zeros((2, 2, 8, 128), F32)

        @pl.when(r == ROWS - 1)
        def _():
            ext[:, 3, 1:3] = jnp.zeros((8, 2, 32, 128), BF)
            halo[:, 2] = jnp.zeros((2, 2, 8, 128), F32)

        @pl.when(c == 0)
        def _():
            halo[0] = jnp.zeros((3, 2, 8, 128), F32)

        @pl.when(c == COLS - 1)
        def _():
            halo[1] = jnp.zeros((3, 2, 8, 128), F32)

        place = lax.broadcasted_iota(jnp.int32, (32, 128), 0)

        def one(s):
            for row, (slot, a) in enumerate(((0, 1), (1, 0), (1, 1), (2, 0))):
                odd = ext[s, row, 2].astype(F32)
                even = ext[s, row, 1].astype(F32)
                before = halo[0, slot, a, pl.ds(s, 1), :]
                after = halo[1, slot, a, pl.ds(s, 1), :]
                ext[s, row, 0] = jnp.where(place == 0, before, pltpu.roll(odd, 1, axis=0)).astype(BF)
                ext[s, row, 3] = jnp.where(place == 31, after, pltpu.roll(even, 31, axis=0)).astype(BF)

        loop(0, 8, one)

    esem = [sems.at[48 + i] for i in range(8)]

    def early_put(at, value):
        n = value.shape[0] // 16
        eg[at // 64, at % 64 : at % 64 + n] = value.astype(BF).reshape(n, 16, 128)

    def early_halves():
        return remote(eg.at[1 - par], epin, esem[0], esem[1], mate, c)

    def early_scatter():
        early_halves().wait()
        ehs[...] = (eg[par].astype(F32) + epin[...].astype(F32)).astype(BF)
        to_parity(0, 8, lambda at, dc: ehs.at[at * COLS + dc], ersin.at[kslot], esem[2], esem[3])

    def early_gather():
        drain(ersin, esem[3])
        eag[par, kslot] = jnp.sum(ersin[...].astype(F32), axis=0).astype(BF)
        mine = eag.at[par, kslot]
        for j in range(1, COLS):
            remote(mine, mine, esem[4], esem[5], r, cols[j]).start()
        def row(i):
            dr = 2 * pair_at(i) + par
            for j in range(COLS):
                remote(mine, mine, esem[4], esem[5], dr, cols[j]).start()

        loop(1, 8, row)

    def early_swap():
        return remote(eag.at[par], eag.at[par], esem[6], esem[7], mate, c)

    def early_drain():
        drain(eag.at[0, pl.ds(0, 63)], esem[5])
        drain(ersin.at[pl.ds(0, 63)], esem[4])
        drain(ehs.at[pl.ds(0, 63)], esem[2])

    low_lane = lax.broadcasted_iota(jnp.int32, (BLOCK, 128), 1) < 64

    def half_turn(value):
        return pltpu.roll(value, 64, axis=1)

    def fold_low(value):
        cut = value.reshape(8, 32, 128)
        first, second = cut[:, 0:16].reshape(128, 128), cut[:, 16:32].reshape(128, 128)
        return jnp.where(low_lane[0:128], first, half_turn(second)).reshape(8, 16, 128)

    def fold_high(value):
        cut = value.reshape(8, 32, 128)
        first, second = cut[:, 0:16].reshape(128, 128), cut[:, 16:32].reshape(128, 128)
        return jnp.where(low_lane[0:128], half_turn(first), second).reshape(8, 16, 128)

    def unfold(src, dst, high, clear):
        def some(i):
            at = pl.ds(8 * i, 8)
            flat = src[at].reshape(128, 128).astype(F32)
            turned = half_turn(flat)
            first, second = (turned, flat) if high else (flat, turned)
            if clear:
                keep = jnp.logical_not(low_lane[0:128]) if high else low_lane[0:128]
                first, second = jnp.where(keep, first, 0.0), jnp.where(keep, second, 0.0)
            dst[at, 0:16] = first.astype(BF).reshape(8, 16, 128)
            dst[at, 16:32] = second.astype(BF).reshape(8, 16, 128)

        loop(0, 4, some)

    loads[0].wait()
    loads[1].wait()
    zero64 = jnp.zeros((64, 256), BF)
    for h in range(HEADS):
        wq[128 * h : 128 * h + 64] = (wqkv[64 * h : 64 * h + 64].astype(F32) * 0.125).astype(BF)
        wq[128 * h + 64 : 128 * h + 128] = zero64
        wkv[128 * h : 128 * h + 64] = wqkv[256 + 64 * h : 320 + 64 * h]
        wkv[128 * h + 64 : 128 * h + 128] = wqkv[512 + 64 * h : 576 + 64 * h]
    xt = x_ref[...].reshape(256, 256)
    for h in range(HEADS):
        rows = slice(128 * h, 128 * h + 128)
        kv = nt(xt, wkv[rows, :]).astype(BF).reshape(8, 32, 128)
        q = fold_low(nt(xt, wq[rows, :])).astype(BF)
        for s in range(8):
            kv_send[s * HEADS + h] = kv[s]
            q_send[s * HEADS + h] = q[s]

    to = lax.broadcasted_iota(jnp.int32, (128, 128), 0)
    of = lax.broadcasted_iota(jnp.int32, (128, 128), 1)
    split = (of == (lax.div(to, 64) * 64 + 2 * lax.rem(to, 32) + lax.rem(lax.div(to, 32), 2))).astype(BF)
    merge = (to == (lax.div(of, 64) * 64 + 2 * lax.rem(of, 32) + lax.rem(lax.div(of, 32), 2))).astype(BF)
    eye = (to == of).astype(BF)

    def take_cot(s):
        g = nn(split, cot_ref[s])
        low = g.astype(BF)
        gx[s, 1:3, 1:3] = low.reshape(2, 2, 32, 128)
        gt[s] = nt(eye, low).astype(BF)
        for a in range(2):
            gedge[0, a, pl.ds(s, 1), :] = g[64 * a : 64 * a + 1]
            gedge[1, a, pl.ds(s, 1), :] = g[64 * a + 63 : 64 * a + 64]

    pl.semaphore_wait(barrier, ROWS * COLS - 1)
    to_attention(q_send, q_fold, sems.at[2], sems.at[3])
    to_parity(
        0, 8, lambda at, dc: kv_send.at[dc * HEADS + lax.div(at, 2)], kv_in.at[par, kslot], sems.at[0],
        lambda i: sems.at[80 + i],
    )
    loads[2].wait()
    loop(0, 8, take_cot)
    cot_copies = halo_start(gx, gedge, ghalo, 16)
    for load in loads[3:]:
        load.wait()

    def take_skip(s):
        pre_ref[s] = nn(split, skip_ref[s])

    loop(0, 8, take_skip)
    for g in range(2):
        block = wout[:, 128 * g : 128 * (g + 1)].astype(F32)
        woutn[:, 256 * g : 256 * g + 128] = jnp.where(low_lane, 0.0, half_turn(block)).astype(BF)
        woutn[:, 256 * g + 128 : 256 * g + 256] = jnp.where(low_lane, 0.0, block).astype(BF)

    def back_conv(half):
        total = jnp.zeros((512, 128), F32)
        for t, (dr, dc) in enumerate(TAPS):
            window = gx[pl.ds(4 * half, 4), 1 - dr : 3 - dr, 1 - dc : 3 - dc].reshape(512, 128)
            total = total + nn(window, wconv[t])
        dh_ref[pl.ds(4 * half, 4)] = total.reshape(4, 128, 128)

    drain(q_fold, sems.at[3])
    unfold(q_fold, q_in, False, True)
    top_ref[...] = jnp.full((1024, 128), -jnp.inf, F32)

    def score(groups):
        parts = []
        for half, at in groups:
            part = kv_in[half, pl.ds(COLS * at, COLS)].reshape(256, 128)
            place = pl.multiple_of(half * 2048 + at * 256, 256)
            v1[pl.ds(place, 256), :] = jnp.where(low_lane, jnp.ones_like(part), part)
            parts.append((part, place))
        for b in range(4):
            rows = slice(BLOCK * b, BLOCK * (b + 1))
            q = q_in[8 * b : 8 * b + 8].reshape(BLOCK, 128)
            top = top_ref[rows, :]
            for part, place in parts:
                s = nt(q, part)
                s_ref[rows, pl.ds(place, 256)] = s
                top = jnp.maximum(top, jnp.maximum(s[:, 0:128], s[:, 128:256]))
            top_ref[rows, :] = top

    def mate_group(i):
        at = kv_in.at[par, pl.ds(COLS * lax.rem(pair + 8 - sign * i, 8), COLS)]
        return remote(at, at, sems.at[88 + i], sems.at[96 + i], mate, c)

    def own_at(i):
        return lax.rem(pair + 8 - sign * i, 8)

    def take_group(i):
        drain(kv_in.at[par, pl.ds(COLS * own_at(i), COLS)], sems.at[80 + i])
        mate_group(i).start()

    take_group(0)
    score([(par, own_at(0))])

    def both(i):
        take_group(i)
        mate_group(i - 1).wait()
        score([(par, own_at(i)), (1 - par, pair_at(i - 1))])

    loop(1, 8, both)
    mate_group(7).wait()
    score([(1 - par, pair_at(7))])
    for _ in range(3):
        drain(kv_send.at[pl.ds(0, 21)], sems.at[0])
    drain32(q_send, sems.at[2])

    def forward(b):
        rows = pl.ds(pl.multiple_of(b * BLOCK, BLOCK), BLOCK)
        m = jnp.max(top_ref[rows, :], axis=1, keepdims=True)
        acc = jnp.zeros((BLOCK, 128), F32)
        for j in range(4096 // 512):
            p = jnp.exp(s_ref[rows, 512 * j : 512 * (j + 1)] - m).astype(BF)
            p_ref[rows, 512 * j : 512 * (j + 1)] = p
            acc = acc + nn(p, v1[512 * j : 512 * (j + 1), :])
        inv = 1.0 / jnp.where(low_lane, 1.0, half_turn(acc))
        invl_ref[rows, :] = inv
        o = jnp.where(low_lane, 0.0, acc * inv)
        o_buf[rows, :] = o.astype(BF)
        o_send[pl.ds(8 * b, 8)] = fold_high(o).astype(BF)
        to_cells(o_send, o_fold, sems.at[6], sems.at[7], b)

    loop(0, 1024 // BLOCK, forward)
    to_parity(0, 8, lambda at, dc: x_ref.at[dc], xall.at[kslot], sems.at[60], sems.at[61], 0, 4)
    halo_finish(gx, ghalo, cot_copies)
    loop(0, 2, back_conv)

    levels = fscale.shape[0]
    level = lax.broadcasted_iota(jnp.int32, (levels, 128), 0)
    scales, shifts = [], []
    for s in range(8):
        here = level == noise[s]
        scales.append(1.0 + jnp.sum(jnp.where(here, fscale[...], 0.0), axis=0, keepdims=True))
        shifts.append(jnp.sum(jnp.where(here, fshift[...], 0.0), axis=0, keepdims=True))
    drain(o_fold, sems.at[7])
    drain32(o_send, sems.at[6])
    unfold(o_fold, ocell, True, False)
    oc = ocell[...].reshape(8, HEADS, 32, 128)
    branch = x_ref[...].reshape(256, 256).astype(F32)
    for h in range(HEADS):
        branch = branch + nt(oc[:, h].reshape(256, 128), woutn[:, 128 * h : 128 * (h + 1)])
    y = branch.astype(BF)
    lifted = nt(y, wup[...])
    for s in range(8):
        u = lifted[32 * s : 32 * (s + 1)]
        pre = pre_ref[s] + jnp.concatenate([u, u, u, u], axis=0)
        pre_ref[s] = pre
        act = pre * scales[s] + shifts[s]
        act_ref[s] = act
        low = (act * jax.nn.sigmoid(act)).astype(BF)
        hx[s, 1:3, 1:3] = low.reshape(2, 2, 32, 128)
        wide = low.astype(F32)
        for a in range(2):
            hedge[0, a, s : s + 1, :] = wide[64 * a : 64 * a + 1]
            hedge[1, a, s : s + 1, :] = wide[64 * a + 63 : 64 * a + 64]
    hid_copies = halo_start(hx, hedge, hhalo, 32)

    spread = lax.broadcasted_iota(jnp.int32, (32, 128), 0)
    scale_sum, shift_sum = jnp.zeros((32, 128), F32), jnp.zeros((32, 128), F32)
    for s in range(8):
        act = act_ref[s]
        sg = jax.nn.sigmoid(act)
        dact = dh_ref[s] * (sg * (1.0 + act * (1.0 - sg)))
        here = spread == noise[s]
        scale_sum += jnp.where(here, jnp.sum(dact * pre_ref[s], axis=0, keepdims=True), 0.0)
        shift_sum += jnp.where(here, jnp.sum(dact, axis=0, keepdims=True), 0.0)
        dpre = dact * scales[s]
        dh_ref[s] = dpre
        du_ref[32 * s : 32 * (s + 1)] = dpre[0:32] + dpre[32:64] + dpre[64:96] + dpre[96:128]
    du = du_ref[...].astype(BF)
    dy = nn(du, wup[...])
    dy_ref[...] = dy
    low_dy = dy.astype(BF)
    for h in range(HEADS):
        do = fold_high(nn(low_dy, woutn[:, 128 * h : 128 * (h + 1)])).astype(BF)
        for s in range(8):
            do_send[s * HEADS + h] = do[s]
    to_attention(do_send, do_fold, sems.at[8], sems.at[9])
    to_parity(0, 8, lambda at, dc: x_ref.at[dc], xall.at[kslot], sems.at[60], sems.at[61], 4, 8)

    early_put(120, scale_sum)
    early_put(122, shift_sum)
    grad_up = nn(du_ref[...].T.astype(BF), y)
    early_put(72, grad_up[:, 0:128])
    early_put(80, grad_up[:, 128:256])
    dyt = dy.T.astype(BF)
    for g in range(2):
        first = nn(dyt, oc[:, 2 * g].reshape(256, 128))
        second = nn(dyt, oc[:, 2 * g + 1].reshape(256, 128))
        early_put(88 + 16 * g, jnp.where(low_lane, half_turn(first), second))

    halo_finish(hx, hhalo, hid_copies)

    def weight_grad(half):
        grads = [gt[4 * half + i] for i in range(4)]
        for t, (dr, dc) in enumerate(TAPS):
            window = hx[pl.ds(4 * half, 4), 1 + dr : 3 + dr, 1 + dc : 3 + dc]
            term = None
            for i in range(4):
                one = nn(grads[i], window[i].reshape(128, 128))
                term = one if term is None else term + one
            gacc[t] = gacc[t] + term

    def conv(half):
        total = jnp.zeros((512, 128), F32)
        for t, (dr, dc) in enumerate(TAPS):
            window = hx[pl.ds(4 * half, 4), 1 + dr : 3 + dr, 1 + dc : 3 + dc]
            total = total + nt(window.reshape(512, 128), wconv[t])
        low = total.astype(BF)
        for i in range(4):
            dec_ref[4 * half + i] = nn(merge, low[128 * i : 128 * (i + 1)]).astype(BF)
            gskip_ref[4 * half + i] = nn(merge, dh_ref[4 * half + i].astype(BF)).astype(BF)

    gacc[...] = jnp.zeros((9, 128, 128), F32)
    loop(0, 2, weight_grad)

    def turn_queries(b):
        q = q_in[pl.ds(8 * b, 8)].reshape(BLOCK, 128)
        qt_ref[b] = q.astype(F32).T[0:64].astype(BF)

    loop(0, 4, turn_queries)
    for t in range(9):
        early_put(8 * t, gacc[t])
    for k in range(124, 128):
        eg[1, k - 64] = jnp.zeros((16, 128), BF)
    early_halves().start()

    drain(do_fold, sems.at[9])
    drain32(do_send, sems.at[8])
    unfold(do_fold, ocell, True, True)
    lane = lax.broadcasted_iota(jnp.int32, (BLOCK, 128), 1)

    def prepare(b):
        rows = pl.ds(pl.multiple_of(b * BLOCK, BLOCK), BLOCK)
        do = (ocell[pl.ds(8 * b, 8)].reshape(BLOCK, 128).astype(F32) * invl_ref[rows, :]).astype(BF)
        dof = do.astype(F32)
        delta = -jnp.sum(dof * o_buf[rows, :].astype(F32), axis=1, keepdims=True)
        high = delta.astype(BF).astype(F32)
        mid = (delta - high).astype(BF).astype(F32)
        rest = delta - high - mid
        ext = jnp.where(lane == 0, high, jnp.where(lane == 1, mid, jnp.where(lane == 2, rest, dof)))
        ext_ref[rows, :] = ext.astype(BF)
        dot_ref[b] = dof.T[64:128].astype(BF)
        dq_acc[rows, :] = jnp.zeros((BLOCK, 128), F32)

    loop(0, 4, prepare)
    gkv[...] = jnp.zeros((256, 256), F32)
    early_scatter()

    def backward(half, j):
        at = pl.multiple_of(half * 2048 + j * CHUNK, CHUNK)
        kc = kv_in[half, pl.ds(32 * j, 32)].reshape(CHUNK, 128)
        vc = v1[pl.ds(at, CHUNK), :]
        for b in range(4):
            rows = slice(BLOCK * b, BLOCK * (b + 1))
            p = p_ref[rows, pl.ds(at, CHUNK)]
            ds = (p.astype(F32) * nt(ext_ref[rows, :], vc)).astype(BF)
            dq_acc[rows, :] += nn(ds, kc)
            for lo, lhs, rhs in ((0, qt_ref, ds), (64, dot_ref, p)):
                part = nn(lhs[b], rhs)
                dkvt[lo : lo + 64] = part if b == 0 else dkvt[lo : lo + 64] + part

    def pair_copy(j):
        return remote(pair_send.at[j], pair_in.at[j], sems.at[10 + j], sems.at[12 + j], mate, c)

    def mate_chunk(j):
        backward(1 - par, j)
        pair_send[j] = dkvt[...].astype(BF)
        pair_copy(j).start()

    loop(0, 2, mate_chunk)

    def own_chunk(j):
        backward(par, j)
        pair_copy(j).wait()
        total = dkvt[...] + pair_in[j].astype(F32)
        dkv_send[pl.ds(32 * j, 32)] = total.T.astype(BF).reshape(32, 32, 128)
        target = dkv_in.at[zhi, spot]

        def row(i):
            rp = 4 * j + lax.rem(pair + i, 4)
            dr = 2 * rp + par
            send_or_keep(rp == pair, dkv_send.at[rp * COLS + c], target, sems.at[14], sems.at[15], dr, c)
            for k in range(1, COLS):
                remote(dkv_send.at[rp * COLS + cols[k]], target, sems.at[14], sems.at[15], dr, cols[k]).start()

        loop(0, 4, row)
        pair_send[j] = total.astype(BF)

    loop(0, 2, own_chunk)

    drain(xall, sems.at[61])
    drain(xall.at[pl.ds(0, 63)], sems.at[60])
    gkv[0:128] = nn(pair_send[0], xall[0:32].reshape(CHUNK, 256)) + nn(pair_send[1], xall[32:64].reshape(CHUNK, 256))
    for b in range(4):
        xq = xall[pl.ds(COLS * (4 * zhi + b), COLS)].reshape(BLOCK, 256)
        gkv[128:256] += nn(dq_acc[BLOCK * b : BLOCK * (b + 1), :].T.astype(BF), xq)

    for g in range(2):
        lanes = slice(128 * g, 128 * (g + 1))
        for part, (lo, factor) in enumerate(((128, 0.125), (0, 1.0), (64, 1.0))):
            piece = (gkv[lo : lo + 64, lanes] * factor).astype(BF)
            lg[12 * g + 4 * part : 12 * g + 4 * part + 4] = piece.reshape(4, 16, 128)

    member = quarter * COLS + c
    kind = head * COLS + c

    def send_lg(i):
        dr = HEADS * head + i
        send_or_keep(quarter == i, lg.at[i * COLS + c], lrs.at[member], sems.at[58], sems.at[59], dr, c)
        for j in range(1, COLS):
            remote(lg.at[i * COLS + cols[j]], lrs.at[member], sems.at[58], sems.at[59], dr, cols[j]).start()

    loop(0, 3, send_lg)

    def give_dq(b):
        rows = pl.ds(pl.multiple_of(b * BLOCK, BLOCK), BLOCK)
        dq_send[pl.ds(8 * b, 8)] = fold_low(dq_acc[rows, :]).astype(BF)
        to_cells(dq_send, dq_fold, sems.at[56], sems.at[57], b)

    loop(0, 4, give_dq)
    early_gather()
    loop(0, 2, conv)
    stores = [
        pltpu.make_async_copy(src, dst, sems.at[68 + i])
        for i, (src, dst) in enumerate((
            (dec_ref, dec_hbm), (gskip_ref, gskip_hbm), (gb_ref, gb_hbm), (eag, eag_hbm), (lag, lag_hbm),
        ))
    ]
    stores[0].start()
    stores[1].start()

    @pl.when(quarter < 3)
    def _():
        drain(lrs, sems.at[59])
        mine = lag.at[quarter * 32 + kind]
        lag[quarter * 32 + kind] = jnp.sum(lrs[...].astype(F32), axis=0).astype(BF)
        for j in range(1, COLS):
            remote(mine, mine, sems.at[64], sems.at[65], r, cols[j]).start()

        def row(i):
            dr = 2 * pair_at(i) + par
            for j in range(COLS):
                remote(mine, mine, sems.at[64], sems.at[65], dr, cols[j]).start()

        loop(1, 8, row)

    early_drain()
    last_swap = early_swap()
    last_swap.start()
    drain(dq_fold, sems.at[57])
    drain32(dq_send, sems.at[56])
    unfold(dq_fold, dq_in, False, False)
    drain(dkv_in, sems.at[15])
    drain(dkv_send.at[pl.ds(0, 63)], sems.at[14])
    dq_all = dq_in[...].reshape(8, HEADS, 32, 128)
    dkv_all = (dkv_in[0].astype(F32) + dkv_in[1].astype(F32)).astype(BF).reshape(8, HEADS, 32, 128)
    grad = dy_ref[...]
    for h in range(HEADS):
        rows = slice(128 * h, 128 * h + 128)
        grad = grad + nn(dq_all[:, h].reshape(256, 128), wq[rows, :])
        grad = grad + nn(dkv_all[:, h].reshape(256, 128), wkv[rows, :])
    gb_ref[...] = grad.reshape(8, 32, 256)
    stores[2].start()
    last_swap.wait()
    stores[3].start()

    @pl.when(quarter < 3)
    def _():
        drain(lg.at[pl.ds(0, 23)], sems.at[58])
        drain(lrs, sems.at[64])
        drain(lrs.at[pl.ds(0, 31)], sems.at[64])

    @pl.when(quarter == 3)
    def _():
        drain(lg, sems.at[58])
        drain(lag.at[pl.ds(0, 32)], sems.at[65])

    @pl.when(quarter == 1)
    def _():
        drain(lag.at[pl.ds(0, 31)], sems.at[65])

    def forward_sums(at):
        part = lag.at[pl.ds(at, 32)]
        remote(part, part, sems.at[66], sems.at[67], mate, c).start()

    @pl.when(par == 0)
    def _():
        drain(lag.at[pl.ds(0, 63)], sems.at[65])
        forward_sums(0)
        forward_sums(64)
        drain(lag.at[pl.ds(0, 64)], sems.at[66])
        drain(lag.at[pl.ds(0, 32)], sems.at[67])

    @pl.when(par == 1)
    def _():
        forward_sums(32)
        drain(lag.at[pl.ds(0, 32)], sems.at[66])
        drain(lag.at[pl.ds(0, 64)], sems.at[67])

    stores[4].start()
    for store in stores:
        store.wait()


def unpack(
    dec, gb, gskip, eag, lag, dec_ref, gb_ref, gskip_ref, gqkv_ref, gout_ref, gup_ref, gconv_ref, gscale_ref, gshift_ref,
    dec_v, gb_v, gskip_v, eag_v, lag_v, gqkv_v, gout_v, gup_v, gconv_v, gscale_v, gshift_v, sems,
):
    held = (dec_v, gb_v, gskip_v, eag_v, lag_v)
    loads = [
        pltpu.make_async_copy(src, dst, sems.at[i]) for i, (src, dst) in enumerate(zip((dec, gb, gskip, eag, lag), held))
    ]
    for load in loads:
        load.start()
    stores = [
        pltpu.make_async_copy(src, dst, sems.at[5 + i])
        for i, (src, dst) in enumerate((
            (dec_v, dec_ref), (gb_v, gb_ref), (gskip_v, gskip_ref), (gconv_v, gconv_ref), (gscale_v, gscale_ref),
            (gshift_v, gshift_ref), (gup_v, gup_ref), (gout_v, gout_ref), (gqkv_v, gqkv_ref),
        ))
    ]
    for i in range(3):
        loads[i].wait()
        stores[i].start()
    loads[3].wait()

    def early(at, n):
        return eag_v[at // 64, at % 64 : at % 64 + n].reshape(n * 16, 128).astype(F32)

    for t in range(9):
        gconv_v[t] = early(8 * t, 8)
    stores[3].start()
    levels = gscale_v.shape[0]
    gscale_v[...] = early(120, 2)[0:levels]
    gshift_v[...] = early(122, 2)[0:levels]
    for g in range(2):
        lanes = slice(128 * g, 128 * (g + 1))
        gup_v[:, lanes] = early(72 + 8 * g, 8)
        gout_v[:, lanes] = early(88 + 16 * g, 16)
    for i in range(4, 8):
        stores[i].start()
    loads[4].wait()
    for g in range(2):
        lanes = slice(128 * g, 128 * (g + 1))
        for part in range(3):
            for h in range(HEADS):
                piece = 12 * g + 4 * part
                at = 32 * (piece // 8) + 8 * h + piece % 8
                rows = slice(256 * part + 64 * h, 256 * part + 64 * h + 64)
                gqkv_v[rows, lanes] = lag_v[at : at + 4].reshape(64, 128).astype(F32)
    stores[8].start()
    for store in stores:
        store.wait()


def on_device(
    bottleneck, skip_field, cotangent, noise_level, qkv_weight, out_weight, up_weight, conv_weight,
    film_scale, film_shift,
):
    levels = film_scale.shape[0]
    x = jnp.transpose(bottleneck, (0, 2, 3, 1)).reshape(8, 32, 256)
    skip = jnp.transpose(skip_field, (0, 2, 3, 1)).reshape(8, 128, 128)
    cot = jnp.transpose(cotangent, (0, 2, 3, 1)).reshape(8, 128, 128)

    def shape(*dims, kind=F32):
        return jax.ShapeDtypeStruct(dims, kind)

    def bf(*dims):
        return pltpu.VMEM(dims, BF)

    def f32(*dims):
        return pltpu.VMEM(dims, F32)

    packet, folded = (32, 32, 128), (32, 16, 128)
    cells, packed = shape(8, 128, 128, kind=BF), shape(8, 32, 256)
    parts = pl.pallas_call(
        kernel,
        out_shape=(cells, packed, cells, shape(2, 64, 16, 128, kind=BF), shape(96, 16, 128, kind=BF)),
        in_specs=[ANY] * 10,
        out_specs=(ANY,) * 5,
        scratch_shapes=[
            bf(8, 128, 128), f32(8, 32, 256), bf(8, 128, 128), bf(2, 64, 16, 128), bf(96, 16, 128),
            pltpu.SMEM((8,), jnp.int32), bf(8, 32, 256), bf(8, 128, 128), bf(8, 128, 128), bf(768, 256), bf(256, 256),
            bf(128, 256), bf(9, 128, 128), f32(levels, 128), f32(levels, 128),
            bf(256, 512), bf(512, 256), bf(512, 256), bf(*packet), bf(*folded), bf(2, 64, 32, 128), bf(*folded),
            bf(*packet), bf(4096, 128), bf(64, 32, 256), f32(1024, 4096), f32(1024, 128), bf(1024, 4096), f32(1024, 128),
            bf(1024, 128), bf(*folded), bf(*folded),
            bf(*packet), bf(8, 4, 4, 32, 128), bf(8, 4, 4, 32, 128), bf(8, 128, 128),
            f32(2, 2, 8, 128), f32(2, 2, 8, 128), f32(2, 3, 2, 8, 128), f32(2, 3, 2, 8, 128),
            f32(8, 128, 128), f32(8, 128, 128), f32(8, 128, 128), f32(256, 256), f32(256, 128),
            bf(*folded), bf(*folded), bf(1024, 128), bf(4, 64, 256), bf(4, 64, 256), f32(128, CHUNK),
            f32(1024, 128), bf(*folded), bf(*folded), bf(*packet),
            bf(2, 128, CHUNK), bf(2, 128, CHUNK), bf(64, 32, 128), bf(2, 32, 32, 128), f32(9, 128, 128), f32(256, 256),
            bf(2, 64, 16, 128), bf(64, 16, 128), bf(64, 16, 128), bf(64, 16, 128),
            bf(24, 16, 128), bf(32, 16, 128),
            pltpu.SemaphoreType.DMA((120,)),
        ],
        compiler_params=pltpu.CompilerParams(
            collective_id=0, has_side_effects=True, vmem_limit_bytes=54 * 1024 * 1024
        ),
        name="unet_step",
    )(noise_level, x, skip, cot, qkv_weight, out_weight, up_weight, conv_weight, film_scale, film_shift)
    outs = pl.pallas_call(
        unpack,
        out_shape=(
            cells, packed, cells, shape(768, 256), shape(256, 256), shape(128, 256), shape(9, 128, 128),
            shape(levels, 128), shape(levels, 128),
        ),
        in_specs=[ANY] * 5,
        out_specs=(ANY,) * 9,
        scratch_shapes=[
            bf(8, 128, 128), f32(8, 32, 256), bf(8, 128, 128), bf(2, 64, 16, 128), bf(96, 16, 128), f32(768, 256),
            f32(256, 256), f32(128, 256), f32(9, 128, 128), f32(levels, 128), f32(levels, 128),
            pltpu.SemaphoreType.DMA((14,)),
        ],
        compiler_params=pltpu.CompilerParams(vmem_limit_bytes=62 * 1024 * 1024),
        name="unpack",
    )(*parts)
    decoded, grad_x, grad_skip = outs[:3]
    return (
        jnp.transpose(decoded.reshape(8, 2, 64, 128), (0, 3, 1, 2)),
        jnp.transpose(grad_x.reshape(8, 1, 32, 256), (0, 3, 1, 2)),
        jnp.transpose(grad_skip.reshape(8, 2, 64, 128), (0, 3, 1, 2)),
    ) + tuple(outs[3:])


def solution(mesh):
    cells = P(None, None, "rows", "cols")
    return jax.shard_map(
        on_device,
        mesh=mesh,
        in_specs=(cells, cells, cells) + (P(),) * 7,
        out_specs=(cells, cells, cells) + (P(),) * 6,
        check_vma=False,
    )
```
